32 devices in a mesh: dates: 2 (over y), ctx: 16 (over z, x, core).
Axes of the slice: x: 2, y: 2, z: 4, core: 2. Of those that a mesh axis runs over, the one named last changes fastest.
Arguments:
- queries: bfloat16 [16384, 2048], P(('dates', 'ctx')), parts along dimension 0, may hold values from -6 to 6
- key_projection_rows: bfloat16 [16384, 1024], P(('dates', 'ctx')), parts along dimension 0, may hold values from -6 to 6
- value_projection_rows: bfloat16 [16384, 1024], P(('dates', 'ctx')), parts along dimension 0, may hold values from -6 to 6
- query_gain: float32 [256], replicated, may hold values from 0.5 to 1.5
- key_norm_gain: float32 [256], replicated, may hold values from 0.5 to 1.5
- session_flags: int32 [16384], P(('dates', 'ctx')), parts along dimension 0, may hold values from 0 to 1, as said below
- valid_length: int32 [2], P('dates'), parts along dimension 0, may hold values from 7936 to 8192
Outputs:
- attended: bfloat16 [16384, 2048], P(('dates', 'ctx')), parts along dimension 0
The draws below stay inside these ranges and needn't reach their ends.
There are 2 independent parts, one for each index of `dates`. The reference program is written for one: setup_inputs(seed, part) draws one part's arguments, and reference() takes and returns one part's arrays. A program takes and returns all parts, laid end to end along the dimension named above; an argument that names none is the same for every part. Nothing has to cross between parts.
Inputs may be any that keep to these rules, and one draw needn't show every extreme that they name: `session_flags`: a 1 marks the first tick of a session; tick 0 always begins one; the ticks of some devices hold no session start.
All inputs are finite; a program needn't handle non-finite values.
Results may differ from the reference program's by a relative error of at most 0.012.
Values may be sent and summed in bfloat16 or wider, within the bound.
A program may use at most 128 MiB of HBM per device.

```python
import jax
import jax.numpy as jnp
from jax import lax

QUERY_HEADS = 8
KEY_VALUE_HEADS = 4
HEAD_DIMENSION = 256
WINDOW_TICKS = 1024
TOK_DEV = 512
CONTEXT_TICKS = 8192


def draw_session_flags(key, part):
    positions = jnp.arange(CONTEXT_TICKS, dtype=jnp.int32)
    owners = positions // TOK_DEV
    within = positions % TOK_DEV
    phase = owners % 4
    random_marks = jax.random.randint(key, (CONTEXT_TICKS,), 0, 2 * TOK_DEV) == 0
    forced = ((phase == 0) | (phase == 3)) & (within == TOK_DEV - 1)
    cleared = (phase == 0) | (phase == 1)
    flags = jnp.where(cleared, False, random_marks) | forced | (positions == 0)
    return flags.astype(jnp.int32)


def steps_of(stream_key, dims, cuts, least, top_value):
    def one(dim, parts):
        heights = jax.random.uniform(jax.random.fold_in(jax.random.fold_in(stream_key, 6), dim), (parts,), jnp.float32, least / len(cuts), top_value / len(cuts))
        return jnp.repeat(jnp.exp(heights), dims[dim] // parts).reshape((-1,) + (1,) * (len(dims) - dim - 1))

    loudness = one(*cuts[0])
    for cut in cuts[1:]:
        loudness = loudness * one(*cut)
    return loudness


def bell_draw(rng, shape, scale, bound, pieces=(), held_as=jnp.bfloat16):
    level = steps_of(rng, shape, pieces, -0.22, 0.18) if pieces else 1.0
    drawn = jax.random.normal(rng, shape, jnp.float32) * scale * level
    return jnp.minimum(jnp.maximum(drawn, -bound), bound).astype(held_as)


def setup_inputs(seed: int = 0, part: int = 0) -> dict:
    key_of = jax.random.split(jax.random.key(seed), 8)
    own_keys = jax.random.split(jax.random.fold_in(key_of[7], part), 8)
    queries = bell_draw(own_keys[0], (CONTEXT_TICKS, QUERY_HEADS * HEAD_DIMENSION), 1.0, 6.0, ((0, 16),))
    key_projection_rows = bell_draw(own_keys[1], (CONTEXT_TICKS, KEY_VALUE_HEADS * HEAD_DIMENSION), 1.0, 6.0, ((0, 16),))
    value_projection_rows = bell_draw(own_keys[2], (CONTEXT_TICKS, KEY_VALUE_HEADS * HEAD_DIMENSION), 1.0, 6.0, ((0, 16),))
    query_gain = jnp.clip(1.0 + 0.1 * jax.random.normal(key_of[3], (HEAD_DIMENSION,), jnp.float32), 0.5, 1.5)
    key_norm_gain = jnp.clip(1.0 + 0.1 * jax.random.normal(key_of[4], (HEAD_DIMENSION,), jnp.float32), 0.5, 1.5)
    session_flags = draw_session_flags(jax.random.fold_in(jax.random.fold_in(key_of[7], part), 71), part)
    valid_length = jax.random.randint(own_keys[6], (1,), CONTEXT_TICKS - TOK_DEV // 2, CONTEXT_TICKS + 1).astype(jnp.int32)
    return dict(queries=queries, key_projection_rows=key_projection_rows, value_projection_rows=value_projection_rows, query_gain=query_gain, key_norm_gain=key_norm_gain, session_flags=session_flags, valid_length=valid_length)


def rootmean_rotary(inputs, gain, tick_positions, heads):
    grand_total = inputs.shape[0]
    vectors = inputs.astype(jnp.float32).reshape(grand_total, heads, HEAD_DIMENSION)
    vectors = vectors * lax.rsqrt(lax.optimization_barrier(jnp.mean(vectors * vectors, axis=-1, keepdims=True)) + 1e-06) * gain.astype(jnp.float32)
    half_width = HEAD_DIMENSION // 2
    inverse = 10000.0 ** (-(jnp.arange(half_width, dtype=jnp.float32) * (2.0 / HEAD_DIMENSION)))
    angles = tick_positions.astype(jnp.float32)[:, None, None] * inverse
    cosine = jnp.cos(angles)
    sine = jnp.sin(angles)
    first = vectors[..., :half_width]
    second = vectors[..., half_width:]
    return jnp.concatenate([first * cosine - second * sine, second * cosine + first * sine], axis=-1).astype(jnp.bfloat16)

def attend(query_tile_block, key_tile_block, value_tile_block, query_pos, key_pos, starts, limit):
    block_extent = query_tile_block.shape[0]
    grouped_heads = query_tile_block.reshape(block_extent, KEY_VALUE_HEADS, QUERY_HEADS // KEY_VALUE_HEADS, HEAD_DIMENSION).astype(jnp.float32)
    scores = jnp.einsum('qhgd,khd->hgqk', grouped_heads, key_tile_block.astype(jnp.float32)) * HEAD_DIMENSION ** (-0.5)
    allowed = (key_pos[None, :] <= query_pos[:, None]) & (key_pos[None, :] > query_pos[:, None] - WINDOW_TICKS) & (key_pos[None, :] >= starts[:, None])
    weights = jnp.where(allowed, jnp.exp(scores), jnp.float32(0.0))
    totals = lax.optimization_barrier(jnp.sum(weights, axis=-1))
    rounded = lax.optimization_barrier(weights.astype(jnp.bfloat16)).astype(jnp.float32)
    mixed = jnp.einsum('hgqk,khd->qhgd', rounded, value_tile_block.astype(jnp.float32))
    mixed = mixed / jnp.transpose(totals, (2, 0, 1))[..., None]
    mixed = mixed.reshape(block_extent, QUERY_HEADS * HEAD_DIMENSION)
    mixed = jnp.where((query_pos < limit)[:, None], mixed, jnp.float32(0.0))
    return mixed.astype(jnp.bfloat16)

def reference(queries, key_projection_rows, value_projection_rows, query_gain, key_norm_gain, session_flags, valid_length):
    grand_total = queries.shape[0]
    tick_positions = jnp.arange(grand_total, dtype=jnp.int32)
    normed_q = rootmean_rotary(queries, query_gain, tick_positions, QUERY_HEADS)
    normalized_keys = rootmean_rotary(key_projection_rows, key_norm_gain, tick_positions, KEY_VALUE_HEADS)
    value_tensor3 = value_projection_rows.reshape(grand_total, KEY_VALUE_HEADS, HEAD_DIMENSION)
    padded_key_rows = jnp.concatenate([jnp.zeros((WINDOW_TICKS, KEY_VALUE_HEADS, HEAD_DIMENSION), jnp.bfloat16), normalized_keys], axis=0)
    padded_value_rows = jnp.concatenate([jnp.zeros((WINDOW_TICKS, KEY_VALUE_HEADS, HEAD_DIMENSION), jnp.bfloat16), value_tensor3], axis=0)
    starts = lax.cummax(jnp.where(session_flags == 1, tick_positions, 0).astype(jnp.int32), axis=0)
    limit = valid_length[0]

    def one_block(block_index):
        first_row = (block_index * TOK_DEV).astype(jnp.int32)
        query_tile_block = lax.dynamic_slice_in_dim(normed_q, first_row, TOK_DEV, 0)
        key_tile_block = lax.dynamic_slice_in_dim(padded_key_rows, first_row, WINDOW_TICKS + TOK_DEV, 0)
        value_tile_block = lax.dynamic_slice_in_dim(padded_value_rows, first_row, WINDOW_TICKS + TOK_DEV, 0)
        start_block = lax.dynamic_slice_in_dim(starts, first_row, TOK_DEV, 0)
        query_pos = first_row + jnp.arange(TOK_DEV, dtype=jnp.int32)
        key_pos = first_row - WINDOW_TICKS + jnp.arange(WINDOW_TICKS + TOK_DEV, dtype=jnp.int32)
        return attend(query_tile_block, key_tile_block, value_tile_block, query_pos, key_pos, start_block, limit)
    blocks = lax.map(one_block, jnp.arange(grand_total // TOK_DEV, dtype=jnp.int32))
    return blocks.reshape(grand_total, QUERY_HEADS * HEAD_DIMENSION)
```

```python
import functools

import jax
import jax.numpy as jnp
import numpy as np
from jax import lax
from jax.experimental import pallas as pl
from jax.experimental.pallas import tpu as pltpu
from jax.sharding import PartitionSpec as P

QUERY_HEADS = 8
KEY_VALUE_HEADS = 4
HEAD = 256
HALF = HEAD // 2
WINDOW = 1024
ROWS = 512
SUB = 256
MESH = pl.DeviceIdType.MESH

PIECES = (
    ("v", 256, 256),
    ("k", 256, 256),
    ("k", 0, 256),
    ("v", 128, 128),
    ("v", 64, 64),
    ("v", 0, 64),
)


def kernel(
    count,
    q_hbm,
    k_hbm,
    v_hbm,
    q_gain_hbm,
    k_gain_hbm,
    flags_hbm,
    rope_hbm,
    valid,
    o_ref,
    q_in,
    k_in,
    rope,
    q_gain,
    k_gain,
    kbuf,
    vbuf,
    qbuf,
    flags,
    low,
    acc,
    total,
    held0,
    held1,
    load_sem,
    fsend_sem,
    frecv_sem,
    i_send,
    i_recv,
    d_send,
    d_recv,
):
    me = lax.axis_index("ctx")
    core = lax.rem(me, 2)
    even, odd = core == 0, core == 1
    chip = me // 2
    chips = count // 2
    near = lax.rem(me + 2, count)
    back = lax.rem(me + count - 2, count)
    partner = me + 1 - 2 * core
    has_after, has_before = chip < chips - 1, chip > 0
    forwards = odd & has_before
    sends_partner = even | has_before
    has_last = me > 0

    barrier = pltpu.get_barrier_semaphore()

    def ready(target):
        pl.semaphore_signal(barrier, inc=1, device_id={"ctx": target}, device_id_type=MESH)

    pl.when(has_before)(lambda: ready(back))
    ready(partner)

    def span(index, width):
        return pl.ds(pl.multiple_of(index * width, width), width)

    def remote(src, dst, send, recv, target):
        return pltpu.make_async_remote_copy(
            src_ref=src,
            dst_ref=dst,
            send_sem=send,
            recv_sem=recv,
            device_id={"ctx": target},
            device_id_type=MESH,
        )

    loads = [
        pltpu.make_async_copy(src, dst, load_sem.at[i])
        for i, (src, dst) in enumerate(
            (
                (rope_hbm, rope),
                (k_hbm, k_in),
                (k_gain_hbm, k_gain),
                (q_hbm, q_in),
                (q_gain_hbm, q_gain),
                (v_hbm, vbuf.at[2]),
                (flags_hbm, flags.at[2]),
            )
        )
    ]
    for copy in loads:
        copy.start()
    load_r, load_k, load_kg, load_q, load_qg, load_v, load_f = loads

    def own(kind, first, rows):
        return (v_hbm if kind == "v" else kbuf.at[2]).at[pl.ds(first, rows)]

    def slot(kind, index, first, rows):
        return (vbuf if kind == "v" else kbuf).at[index, pl.ds(first, rows)]

    to_near, to_partner, forward = [], [], []
    for i, piece in enumerate(PIECES):
        to_near.append(remote(own(*piece), slot(piece[0], 0, *piece[1:]), i_send.at[i], i_recv.at[i], near))
        there = slot(piece[0], 1, *piece[1:])
        to_partner.append(remote(own(*piece), there, d_send.at[i], d_recv.at[i], partner))
        forward.append(
            remote(slot(piece[0], 0, *piece[1:]), there, d_send.at[i], d_recv.at[i], partner)
        )
    flags_near = remote(flags_hbm, flags.at[0], fsend_sem.at[0], frecv_sem.at[0], near)
    flags_partner = remote(flags_hbm, flags.at[1], fsend_sem.at[1], frecv_sem.at[1], partner)
    flags_forward = remote(flags.at[0], flags.at[1], fsend_sem.at[1], frecv_sem.at[1], partner)

    pl.when(has_after)(lambda: pl.semaphore_wait(barrier, 2))
    pl.when(jnp.logical_not(has_after))(lambda: pl.semaphore_wait(barrier, 1))

    def start_all(condition, copies):
        @pl.when(condition)
        def _():
            for copy in copies:
                copy.start()

    start_all(has_after, [flags_near])
    start_all(has_after & odd, to_near[:1])
    start_all(even, [flags_partner] + [to_partner[i] for i in (0, 3, 4, 5)])

    load_r.wait()
    base = (me * ROWS).astype(jnp.float32) * rope[2, :8]
    base_cos, base_sin = jnp.cos(base)[:1], jnp.sin(base)[:1]
    row_cos, row_sin = rope[0], rope[1]
    rope[0] = base_cos * row_cos - base_sin * row_sin
    rope[1] = base_sin * row_cos + base_cos * row_sin

    def normed(raw, gain, rows, scale):
        x = raw.astype(jnp.float32)
        mean = jnp.sum(x * x, axis=-1, keepdims=True) * (1.0 / HEAD)
        x = x * lax.rsqrt(mean + 1e-06) * gain
        a, b = x[:, :HALF], x[:, HALF:]
        cosine, sine = rope[0, rows], rope[1, rows]
        first = (a * cosine - b * sine).astype(jnp.bfloat16)
        second = (b * cosine + a * sine).astype(jnp.bfloat16)
        if scale != 1.0:
            first, second = first * jnp.bfloat16(scale), second * jnp.bfloat16(scale)
        return first, second

    load_k.wait()
    load_kg.wait()
    for i in (1, 2):
        rows = pl.ds(*PIECES[i][1:])
        for h in range(KEY_VALUE_HEADS):
            first, second = normed(k_in[rows, h * HEAD : (h + 1) * HEAD], k_gain[...], rows, 1.0)
            kbuf[2, rows, h * HEAD : h * HEAD + HALF] = first
            kbuf[2, rows, h * HEAD + HALF : (h + 1) * HEAD] = second
        start_all(has_after & odd, to_near[i : i + 1])
        start_all(even, to_partner[i : i + 1])
    start_all(has_after & odd, to_near[3:])

    load_q.wait()
    load_qg.wait()

    def prepare(h, carry):
        for j in range(2):
            for u in range(2):
                rows = pl.ds(u * SUB, SUB)
                raw = q_in[rows, span(h * 2 + j, HEAD)]
                first, second = normed(raw, q_gain[...], rows, HEAD**-0.5)
                qbuf[h, j, rows, :HALF] = first
                qbuf[h, j, rows, HALF:] = second
        return carry

    lax.fori_loop(0, KEY_VALUE_HEADS, prepare, 0)
    start_all(has_after & even, to_near)

    load_f.wait()

    @pl.when(has_before)
    def _():
        flags_near.wait_recv()

    start_all(forwards, [flags_forward])

    @pl.when(has_last)
    def _():
        flags_partner.wait_recv()

    @pl.when(jnp.logical_not(has_before))
    def _():
        flags[0] = jnp.zeros((1, ROWS), jnp.int32)

    @pl.when(jnp.logical_not(has_last))
    def _():
        flags[1] = jnp.zeros((1, ROWS), jnp.int32)

    first_tick = (me - 2) * ROWS
    column = lax.broadcasted_iota(jnp.int32, (1, ROWS), 1)

    def marks(index):
        place = column + index * ROWS
        return jnp.where((flags[index] == 1) & (place + first_tick >= 0), place, -first_tick)

    behind = jnp.max(jnp.maximum(marks(0), marks(1)), axis=1, keepdims=True)
    row = lax.broadcasted_iota(jnp.int32, (ROWS, ROWS), 0)
    col = lax.broadcasted_iota(jnp.int32, (ROWS, ROWS), 1)
    seen = jnp.where(col <= row, jnp.broadcast_to(marks(2), (ROWS, ROWS)), -first_tick)
    start = jnp.maximum(jnp.max(seen, axis=1, keepdims=True), behind)
    tick = lax.broadcasted_iota(jnp.int32, (ROWS, 1), 0) + WINDOW
    low[...] = jnp.broadcast_to(jnp.maximum(start, tick - (WINDOW - 1)), (ROWS, 128))

    def weigh(h, u, index, first, keys):
        ticks = pl.ds(u * SUB, SUB)
        q = qbuf[h, :, ticks, :].reshape(2 * SUB, HEAD)
        k = kbuf[index, pl.ds(first, keys), span(h, HEAD)]
        score = lax.dot_general(q, k, (((1,), (1,)), ((), ())), preferred_element_type=jnp.float32)
        offset = index * ROWS + first
        place = lax.broadcasted_iota(jnp.int32, (SUB, keys), 1) + offset
        allowed = place >= low[ticks][:, :1]
        if index == 2 and first + keys > u * SUB:
            tick = lax.broadcasted_iota(jnp.int32, (SUB, keys), 0) + (WINDOW + u * SUB)
            allowed = allowed & (place <= tick)
        weight = jnp.where(allowed[None], jnp.exp(score).reshape(2, SUB, keys), 0.0)
        weight = weight.reshape(2 * SUB, keys)
        lanes = weight[:, :128]
        for i in range(1, keys // 128):
            lanes = lanes + weight[:, i * 128 : (i + 1) * 128]
        return weight.astype(jnp.bfloat16), lanes.reshape(2, SUB, 128)

    def mix(weight, h, index, first, keys):
        v = vbuf[index, pl.ds(first, keys), span(h, HEAD)]
        mixed = jnp.dot(weight, v, preferred_element_type=jnp.float32)
        return mixed.reshape(2, weight.shape[0] // 2, HEAD)

    def part(h, u, index, first, keys, first_use=False):
        weight, lanes = weigh(h, u, index, first, keys)
        mixed = mix(weight, h, index, first, keys)
        if first_use:
            acc[h, u] = mixed
            total[h, u] = lanes
        else:
            acc[h, u] += mixed
            total[h, u] += lanes

    def each_head(step):
        lax.fori_loop(0, KEY_VALUE_HEADS, lambda h, carry: (step(h), carry)[1], 0)

    load_v.wait()

    def own_part(h):
        part(h, 0, 2, 0, SUB, True)
        part(h, 1, 2, 0, ROWS, True)

    each_head(own_part)

    def receive(pieces):
        @pl.when(forwards)
        def _():
            for i in pieces:
                to_near[i].wait_recv()
                forward[i].start()

        @pl.when(has_last)
        def _():
            for i in pieces:
                to_partner[i].wait_recv()

    def receive_own(pieces):
        @pl.when(has_before & even)
        def _():
            for i in pieces:
                to_near[i].wait_recv()

    receive((0, 1))

    @pl.when(has_last)
    def _():
        def step(h):
            part(h, 0, 1, SUB, SUB)
            part(h, 1, 1, SUB, SUB)

        each_head(step)

    receive_own((0, 1))

    @pl.when(has_before)
    def _():
        def step(h):
            part(h, 0, 0, SUB, SUB)
            part(h, 1, 0, SUB, SUB)

        each_head(step)

    receive((2,))

    @pl.when(has_last)
    def _():
        def step(h):
            for u in range(2):
                weight, lanes = weigh(h, u, 1, 0, SUB)
                held1[h, u] = weight
                total[h, u] += lanes

        each_head(step)

    receive_own((2,))

    @pl.when(has_before)
    def _():
        def step(h):
            weight, lanes = weigh(h, 0, 0, 0, SUB)
            held0[h] = weight.reshape(2, SUB, SUB)
            total[h, 0] += lanes

        each_head(step)

    limit = valid[0]

    def finish(h, u, first, rows):
        ticks = pl.ds(first, rows)
        for j in range(2):
            whole = jnp.sum(total[h, u, j, ticks], axis=-1, keepdims=True)
            place = lax.broadcasted_iota(jnp.int32, (rows, 1), 0) + (me * ROWS + u * SUB + first)
            share = jnp.where(place < limit, 1.0 / whole, 0.0)
            value = (acc[h, u, j, ticks] * share).astype(jnp.bfloat16)
            o_ref[pl.ds(u * SUB + first, rows), span(h * 2 + j, HEAD)] = value

    receive((3, 4, 5))

    @pl.when(has_last)
    def _():
        def step(h):
            for u in range(2):
                acc[h, u] += mix(held1[h, u], h, 1, 0, SUB)

        each_head(step)

    each_head(lambda h: finish(h, 1, 0, SUB))

    for i in (3, 4, 5):
        first, rows = PIECES[i][1:]
        receive_own((i,))

        @pl.when(has_before)
        def _():
            def step(h):
                weight = held0[h, :, pl.ds(0, first + rows), pl.ds(first, rows)]
                weight = weight.reshape(2 * (first + rows), rows)
                acc[h, 0, :, pl.ds(0, first + rows)] += mix(weight, h, 0, first, rows)

            each_head(step)

        each_head(lambda h: finish(h, 0, first, rows))

    @pl.when(has_after)
    def _():
        for copy in [flags_near] + to_near:
            copy.wait_send()

    @pl.when(sends_partner)
    def _():
        for copy in [flags_partner] + to_partner:
            copy.wait_send()


def solution(mesh):
    count = mesh.shape["ctx"]
    inverse = 10000.0 ** (-(np.arange(HALF, dtype=np.float64) * (2.0 / HEAD)))
    angle = np.arange(ROWS, dtype=np.float64)[:, None] * inverse
    table = np.stack([np.cos(angle), np.sin(angle), 0 * angle + inverse]).astype(np.float32)

    def body(queries, keys, values, query_gain, key_gain, session_flags, valid_length):
        assert queries.shape[0] == ROWS and 2 * ROWS == WINDOW
        pinned = functools.partial(pltpu.with_memory_space_constraint, memory_space=pltpu.HBM)
        bf16, f32, i32 = jnp.bfloat16, jnp.float32, jnp.int32
        dma = pltpu.SemaphoreType.DMA
        heads, pieces = KEY_VALUE_HEADS, len(PIECES)
        return pl.pallas_call(
            functools.partial(kernel, count),
            out_shape=pltpu.VMEM((ROWS, QUERY_HEADS * HEAD), bf16),
            in_specs=[pl.BlockSpec(memory_space=pltpu.HBM)] * 7
            + [pl.BlockSpec(memory_space=pltpu.SMEM)],
            out_specs=pl.BlockSpec(memory_space=pltpu.VMEM),
            scratch_shapes=[
                pltpu.VMEM((ROWS, QUERY_HEADS * HEAD), bf16),
                pltpu.VMEM((ROWS, KEY_VALUE_HEADS * HEAD), bf16),
                pltpu.VMEM((3, ROWS, HALF), f32),
                pltpu.VMEM((1, HEAD), f32),
                pltpu.VMEM((1, HEAD), f32),
                pltpu.VMEM((3, ROWS, KEY_VALUE_HEADS * HEAD), bf16),
                pltpu.VMEM((3, ROWS, KEY_VALUE_HEADS * HEAD), bf16),
                pltpu.VMEM((heads, 2, ROWS, HEAD), bf16),
                pltpu.VMEM((3, 1, ROWS), i32),
                pltpu.VMEM((ROWS, 128), i32),
                pltpu.VMEM((heads, 2, 2, SUB, HEAD), f32),
                pltpu.VMEM((heads, 2, 2, SUB, 128), f32),
                pltpu.VMEM((heads, 2, SUB, SUB), bf16),
                pltpu.VMEM((heads, 2, 2 * SUB, SUB), bf16),
                dma((7,)),
                dma((2,)),
                dma((2,)),
                dma((pieces,)),
                dma((pieces,)),
                dma((pieces,)),
                dma((pieces,)),
            ],
            compiler_params=pltpu.CompilerParams(
                collective_id=0, has_side_effects=True, vmem_limit_bytes=56 << 20
            ),
        )(
            pinned(queries),
            pinned(keys),
            pinned(values),
            pinned(query_gain.reshape(1, HEAD)),
            pinned(key_gain.reshape(1, HEAD)),
            pinned(session_flags.reshape(1, ROWS)),
            pinned(jnp.asarray(table)),
            valid_length,
        )

    return jax.shard_map(
        body,
        mesh=mesh,
        in_specs=(
            P(("dates", "ctx"), None),
            P(("dates", "ctx"), None),
            P(("dates", "ctx"), None),
            P(),
            P(),
            P(("dates", "ctx")),
            P("dates"),
        ),
        out_specs=P(("dates", "ctx"), None),
        check_vma=False,
    )
```

```python
import functools

import jax
import jax.numpy as jnp
import numpy as np
from jax import lax
from jax.experimental import pallas as pl
from jax.experimental.pallas import tpu as pltpu
from jax.sharding import PartitionSpec as P

QUERY_HEADS = 8
KEY_VALUE_HEADS = 4
HEAD = 256
HALF = HEAD // 2
WINDOW = 1024
ROWS = 512
SUB = 256
MESH = pl.DeviceIdType.MESH

PIECES = (
    ("v", 256, 256),
    ("k", 256, 256),
    ("k", 0, 256),
    ("v", 128, 128),
    ("v", 64, 64),
    ("v", 0, 64),
)


def kernel(
    count,
    q_hbm,
    k_hbm,
    v_hbm,
    q_gain_hbm,
    k_gain_hbm,
    flags_hbm,
    rope_hbm,
    valid,
    o_ref,
    q_in,
    k_in,
    rope,
    q_gain,
    k_gain,
    kbuf,
    vbuf,
    qbuf,
    flags,
    low,
    acc,
    total,
    held0,
    held1,
    load_sem,
    fsend_sem,
    frecv_sem,
    i_send,
    i_recv,
    d_send,
    d_recv,
):
    me = lax.axis_index("ctx")
    core = lax.rem(me, 2)
    even, odd = core == 0, core == 1
    chip = me // 2
    chips = count // 2
    near = lax.rem(me + 2, count)
    back = lax.rem(me + count - 2, count)
    partner = me + 1 - 2 * core
    has_after, has_before = chip < chips - 1, chip > 0
    forwards = odd & has_before
    sends_partner = even | has_before
    has_last = me > 0

    barrier = pltpu.get_barrier_semaphore()

    def ready(target):
        pl.semaphore_signal(barrier, inc=1, device_id={"ctx": target}, device_id_type=MESH)

    pl.when(has_before)(lambda: ready(back))
    ready(partner)

    def span(index, width):
        return pl.ds(pl.multiple_of(index * width, width), width)

    def remote(src, dst, send, recv, target):
        return pltpu.make_async_remote_copy(
            src_ref=src,
            dst_ref=dst,
            send_sem=send,
            recv_sem=recv,
            device_id={"ctx": target},
            device_id_type=MESH,
        )

    loads = [
        pltpu.make_async_copy(src, dst, load_sem.at[i])
        for i, (src, dst) in enumerate(
            (
                (rope_hbm, rope),
                (k_hbm, k_in),
                (k_gain_hbm, k_gain),
                (q_hbm, q_in),
                (q_gain_hbm, q_gain),
                (v_hbm, vbuf.at[2]),
                (flags_hbm, flags.at[2]),
            )
        )
    ]
    for copy in loads:
        copy.start()
    load_r, load_k, load_kg, load_q, load_qg, load_v, load_f = loads

    def own(kind, first, rows):
        return (v_hbm if kind == "v" else kbuf.at[2]).at[pl.ds(first, rows)]

    def slot(kind, index, first, rows):
        return (vbuf if kind == "v" else kbuf).at[index, pl.ds(first, rows)]

    to_near, to_partner, forward = [], [], []
    for i, piece in enumerate(PIECES):
        to_near.append(remote(own(*piece), slot(piece[0], 0, *piece[1:]), i_send.at[i], i_recv.at[i], near))
        there = slot(piece[0], 1, *piece[1:])
        to_partner.append(remote(own(*piece), there, d_send.at[i], d_recv.at[i], partner))
        forward.append(
            remote(slot(piece[0], 0, *piece[1:]), there, d_send.at[i], d_recv.at[i], partner)
        )
    flags_near = remote(flags_hbm, flags.at[0], fsend_sem.at[0], frecv_sem.at[0], near)
    flags_partner = remote(flags_hbm, flags.at[1], fsend_sem.at[1], frecv_sem.at[1], partner)
    flags_forward = remote(flags.at[0], flags.at[1], fsend_sem.at[1], frecv_sem.at[1], partner)

    pl.when(has_after)(lambda: pl.semaphore_wait(barrier, 2))
    pl.when(jnp.logical_not(has_after))(lambda: pl.semaphore_wait(barrier, 1))

    def start_all(condition, copies):
        @pl.when(condition)
        def _():
            for copy in copies:
                copy.start()

    start_all(has_after, [flags_near])
    start_all(has_after & odd, to_near[:1])
    start_all(even, [flags_partner] + [to_partner[i] for i in (0, 3, 4, 5)])

    load_r.wait()
    base = (me * ROWS).astype(jnp.float32) * rope[2, :8]
    base_cos, base_sin = jnp.cos(base)[:1], jnp.sin(base)[:1]
    row_cos, row_sin = rope[0], rope[1]
    rope[0] = base_cos * row_cos - base_sin * row_sin
    rope[1] = base_sin * row_cos + base_cos * row_sin

    def normed(raw, gain, rows, scale):
        x = raw.astype(jnp.float32)
        mean = jnp.sum(x * x, axis=-1, keepdims=True) * (1.0 / HEAD)
        x = x * lax.rsqrt(mean + 1e-06) * gain
        a, b = x[:, :HALF], x[:, HALF:]
        cosine, sine = rope[0, rows], rope[1, rows]
        first = (a * cosine - b * sine).astype(jnp.bfloat16)
        second = (b * cosine + a * sine).astype(jnp.bfloat16)
        if scale != 1.0:
            first, second = first * jnp.bfloat16(scale), second * jnp.bfloat16(scale)
        return first, second

    load_k.wait()
    load_kg.wait()
    for i in (1, 2):
        rows = pl.ds(*PIECES[i][1:])
        for h in range(KEY_VALUE_HEADS):
            first, second = normed(k_in[rows, h * HEAD : (h + 1) * HEAD], k_gain[...], rows, 1.0)
            kbuf[2, rows, h * HEAD : h * HEAD + HALF] = first
            kbuf[2, rows, h * HEAD + HALF : (h + 1) * HEAD] = second
        start_all(has_after & odd, to_near[i : i + 1])
        start_all(even, to_partner[i : i + 1])
    start_all(has_after & odd, to_near[3:])

    load_q.wait()
    load_qg.wait()

    def prepare(h, carry):
        for j in range(2):
            for u in range(2):
                rows = pl.ds(u * SUB, SUB)
                raw = q_in[rows, span(h * 2 + j, HEAD)]
                first, second = normed(raw, q_gain[...], rows, HEAD**-0.5)
                qbuf[h, j, rows, :HALF] = first
                qbuf[h, j, rows, HALF:] = second
        return carry

    lax.fori_loop(0, KEY_VALUE_HEADS, prepare, 0)

    load_f.wait()

    @pl.when(has_before)
    def _():
        flags_near.wait_recv()

    start_all(forwards, [flags_forward])

    @pl.when(has_last)
    def _():
        flags_partner.wait_recv()

    @pl.when(jnp.logical_not(has_before))
    def _():
        flags[0] = jnp.zeros((1, ROWS), jnp.int32)

    @pl.when(jnp.logical_not(has_last))
    def _():
        flags[1] = jnp.zeros((1, ROWS), jnp.int32)

    first_tick = (me - 2) * ROWS
    column = lax.broadcasted_iota(jnp.int32, (1, ROWS), 1)

    def marks(index):
        place = column + index * ROWS
        return jnp.where((flags[index] == 1) & (place + first_tick >= 0), place, -first_tick)

    behind = jnp.max(jnp.maximum(marks(0), marks(1)), axis=1, keepdims=True)
    row = lax.broadcasted_iota(jnp.int32, (ROWS, ROWS), 0)
    col = lax.broadcasted_iota(jnp.int32, (ROWS, ROWS), 1)
    seen = jnp.where(col <= row, jnp.broadcast_to(marks(2), (ROWS, ROWS)), -first_tick)
    start = jnp.maximum(jnp.max(seen, axis=1, keepdims=True), behind)
    tick = lax.broadcasted_iota(jnp.int32, (ROWS, 1), 0) + WINDOW
    low[...] = jnp.broadcast_to(jnp.maximum(start, tick - (WINDOW - 1)), (ROWS, 128))

    def weigh(h, u, index, first, keys):
        ticks = pl.ds(u * SUB, SUB)
        q = qbuf[h, :, ticks, :].reshape(2 * SUB, HEAD)
        k = kbuf[index, pl.ds(first, keys), span(h, HEAD)]
        score = lax.dot_general(q, k, (((1,), (1,)), ((), ())), preferred_element_type=jnp.float32)
        offset = index * ROWS + first
        place = lax.broadcasted_iota(jnp.int32, (SUB, keys), 1) + offset
        allowed = place >= low[ticks][:, :1]
        if index == 2 and first + keys > u * SUB:
            tick = lax.broadcasted_iota(jnp.int32, (SUB, keys), 0) + (WINDOW + u * SUB)
            allowed = allowed & (place <= tick)
        weight = jnp.where(allowed[None], jnp.exp(score).reshape(2, SUB, keys), 0.0)
        weight = weight.reshape(2 * SUB, keys)
        lanes = weight[:, :128]
        for i in range(1, keys // 128):
            lanes = lanes + weight[:, i * 128 : (i + 1) * 128]
        return weight.astype(jnp.bfloat16), lanes.reshape(2, SUB, 128)

    def mix(weight, h, index, first, keys):
        v = vbuf[index, pl.ds(first, keys), span(h, HEAD)]
        mixed = jnp.dot(weight, v, preferred_element_type=jnp.float32)
        return mixed.reshape(2, weight.shape[0] // 2, HEAD)

    def part(h, u, index, first, keys, first_use=False):
        weight, lanes = weigh(h, u, index, first, keys)
        mixed = mix(weight, h, index, first, keys)
        if first_use:
            acc[h, u] = mixed
            total[h, u] = lanes
        else:
            acc[h, u] += mixed
            total[h, u] += lanes

    def each_head(step):
        lax.fori_loop(0, KEY_VALUE_HEADS, lambda h, carry: (step(h), carry)[1], 0)

    load_v.wait()

    def own_part(h):
        part(h, 0, 2, 0, SUB, True)
        part(h, 1, 2, 0, ROWS, True)

    each_head(own_part)
    start_all(has_after & even, to_near)

    def receive(pieces):
        @pl.when(forwards)
        def _():
            for i in pieces:
                to_near[i].wait_recv()
                forward[i].start()

        @pl.when(has_last)
        def _():
            for i in pieces:
                to_partner[i].wait_recv()

    def receive_own(pieces):
        @pl.when(has_before & even)
        def _():
            for i in pieces:
                to_near[i].wait_recv()

    receive((0, 1))

    @pl.when(has_last)
    def _():
        def step(h):
            part(h, 0, 1, SUB, SUB)
            part(h, 1, 1, SUB, SUB)

        each_head(step)

    receive_own((0, 1))

    @pl.when(has_before)
    def _():
        def step(h):
            part(h, 0, 0, SUB, SUB)
            part(h, 1, 0, SUB, SUB)

        each_head(step)

    receive((2,))

    @pl.when(has_last)
    def _():
        def step(h):
            for u in range(2):
                weight, lanes = weigh(h, u, 1, 0, SUB)
                held1[h, u] = weight
                total[h, u] += lanes

        each_head(step)

    receive_own((2,))

    @pl.when(has_before)
    def _():
        def step(h):
            weight, lanes = weigh(h, 0, 0, 0, SUB)
            held0[h] = weight.reshape(2, SUB, SUB)
            total[h, 0] += lanes

        each_head(step)

    limit = valid[0]

    def divide(h):
        for u in range(2):
            place = lax.broadcasted_iota(jnp.int32, (SUB, 1), 0) + (me * ROWS + u * SUB)
            for j in range(2):
                whole = jnp.sum(total[h, u, j], axis=-1, keepdims=True)
                share = jnp.where(place < limit, 1.0 / whole, 0.0)
                total[h, u, j] = jnp.broadcast_to(share, (SUB, 128))

    each_head(divide)

    def finish(h, u, first, rows, mixed):
        ticks = pl.ds(first, rows)
        for j in range(2):
            share = total[h, u, j, ticks]
            for half in range(2):
                lanes = slice(half * HALF, (half + 1) * HALF)
                value = acc[h, u, j, ticks, lanes]
                if mixed is not None:
                    value = value + mixed[j, :, lanes]
                out = pl.ds(pl.multiple_of((h * 2 + j) * HEAD + half * HALF, HALF), HALF)
                o_ref[pl.ds(u * SUB + first, rows), out] = (value * share).astype(jnp.bfloat16)

    @pl.when(has_last)
    def _():
        for i in (3, 4, 5):
            to_partner[i].wait_recv()

        def step(h):
            acc[h, 0] += mix(held1[h, 0], h, 1, 0, SUB)
            finish(h, 1, 0, SUB, mix(held1[h, 1], h, 1, 0, SUB))

        each_head(step)

    @pl.when(jnp.logical_not(has_last))
    def _():
        each_head(lambda h: finish(h, 1, 0, SUB, None))

    @pl.when(jnp.logical_not(has_before))
    def _():
        each_head(lambda h: finish(h, 0, 0, SUB, None))

    @pl.when(has_before)
    def _():
        for i in (3, 4, 5):
            first, rows = PIECES[i][1:]
            to_near[i].wait_recv()
            pl.when(odd)(forward[i].start)
            for h in range(KEY_VALUE_HEADS):
                weight = held0[h, :, pl.ds(0, first + rows), pl.ds(first, rows)]
                mixed = mix(weight.reshape(2 * (first + rows), rows), h, 0, first, rows)
                if first:
                    acc[h, 0, :, pl.ds(0, first)] += mixed[:, :first]
                finish(h, 0, first, rows, mixed[:, first:])

    @pl.when(has_after)
    def _():
        for copy in [flags_near] + to_near:
            copy.wait_send()

    @pl.when(sends_partner)
    def _():
        for copy in [flags_partner] + to_partner:
            copy.wait_send()


def solution(mesh):
    count = mesh.shape["ctx"]
    inverse = 10000.0 ** (-(np.arange(HALF, dtype=np.float64) * (2.0 / HEAD)))
    angle = np.arange(ROWS, dtype=np.float64)[:, None] * inverse
    table = np.stack([np.cos(angle), np.sin(angle), 0 * angle + inverse]).astype(np.float32)

    def body(queries, keys, values, query_gain, key_gain, session_flags, valid_length):
        assert queries.shape[0] == ROWS and 2 * ROWS == WINDOW
        pinned = functools.partial(pltpu.with_memory_space_constraint, memory_space=pltpu.HBM)
        bf16, f32, i32 = jnp.bfloat16, jnp.float32, jnp.int32
        dma = pltpu.SemaphoreType.DMA
        heads, pieces = KEY_VALUE_HEADS, len(PIECES)
        return pl.pallas_call(
            functools.partial(kernel, count),
            out_shape=pltpu.VMEM((ROWS, QUERY_HEADS * HEAD), bf16),
            in_specs=[pl.BlockSpec(memory_space=pltpu.HBM)] * 7
            + [pl.BlockSpec(memory_space=pltpu.SMEM)],
            out_specs=pl.BlockSpec(memory_space=pltpu.VMEM),
            scratch_shapes=[
                pltpu.VMEM((ROWS, QUERY_HEADS * HEAD), bf16),
                pltpu.VMEM((ROWS, KEY_VALUE_HEADS * HEAD), bf16),
                pltpu.VMEM((3, ROWS, HALF), f32),
                pltpu.VMEM((1, HEAD), f32),
                pltpu.VMEM((1, HEAD), f32),
                pltpu.VMEM((3, ROWS, KEY_VALUE_HEADS * HEAD), bf16),
                pltpu.VMEM((3, ROWS, KEY_VALUE_HEADS * HEAD), bf16),
                pltpu.VMEM((heads, 2, ROWS, HEAD), bf16),
                pltpu.VMEM((3, 1, ROWS), i32),
                pltpu.VMEM((ROWS, 128), i32),
                pltpu.VMEM((heads, 2, 2, SUB, HEAD), f32),
                pltpu.VMEM((heads, 2, 2, SUB, 128), f32),
                pltpu.VMEM((heads, 2, SUB, SUB), bf16),
                pltpu.VMEM((heads, 2, 2 * SUB, SUB), bf16),
                dma((7,)),
                dma((2,)),
                dma((2,)),
                dma((pieces,)),
                dma((pieces,)),
                dma((pieces,)),
                dma((pieces,)),
            ],
            compiler_params=pltpu.CompilerParams(
                collective_id=0, has_side_effects=True, vmem_limit_bytes=56 << 20
            ),
        )(
            pinned(queries),
            pinned(keys),
            pinned(values),
            pinned(query_gain.reshape(1, HEAD)),
            pinned(key_gain.reshape(1, HEAD)),
            pinned(session_flags.reshape(1, ROWS)),
            pinned(jnp.asarray(table)),
            valid_length,
        )

    return jax.shard_map(
        body,
        mesh=mesh,
        in_specs=(
            P(("dates", "ctx"), None),
            P(("dates", "ctx"), None),
            P(("dates", "ctx"), None),
            P(),
            P(),
            P(("dates", "ctx")),
            P("dates"),
        ),
        out_specs=P(("dates", "ctx"), None),
        check_vma=False,
    )
```

```python
import functools

import jax
import jax.numpy as jnp
import numpy as np
from jax import lax
from jax.experimental import pallas as pl
from jax.experimental.pallas import tpu as pltpu
from jax.sharding import PartitionSpec as P

QUERY_HEADS = 8
KEY_VALUE_HEADS = 4
HEAD = 256
HALF = HEAD // 2
WINDOW = 1024
ROWS = 512
SUB = 256
MESH = pl.DeviceIdType.MESH

PIECES = (
    ("v", 256, 256),
    ("k", 256, 256),
    ("k", 0, 256),
    ("v", 128, 128),
    ("v", 64, 64),
    ("v", 0, 64),
)


def kernel(
    count,
    q_hbm,
    k_hbm,
    v_hbm,
    q_gain_hbm,
    k_gain_hbm,
    flags_hbm,
    rope_hbm,
    o_ref,
    q_in,
    k_in,
    rope,
    q_gain,
    k_gain,
    kbuf,
    vbuf,
    qbuf,
    flags,
    low,
    acc,
    total,
    held0,
    held1,
    load_sem,
    fsend_sem,
    frecv_sem,
    i_send,
    i_recv,
    d_send,
    d_recv,
):
    me = lax.axis_index("ctx")
    core = lax.rem(me, 2)
    even, odd = core == 0, core == 1
    chip = me // 2
    chips = count // 2
    near = lax.rem(me + 2, count)
    back = lax.rem(me + count - 2, count)
    partner = me + 1 - 2 * core
    has_after, has_before = chip < chips - 1, chip > 0
    forwards = odd & has_before
    sends_partner = even | has_before
    has_last = me > 0

    barrier = pltpu.get_barrier_semaphore()

    def ready(target):
        pl.semaphore_signal(barrier, inc=1, device_id={"ctx": target}, device_id_type=MESH)

    pl.when(has_before)(lambda: ready(back))
    ready(partner)

    def span(index, width):
        return pl.ds(pl.multiple_of(index * width, width), width)

    def remote(src, dst, send, recv, target):
        return pltpu.make_async_remote_copy(
            src_ref=src,
            dst_ref=dst,
            send_sem=send,
            recv_sem=recv,
            device_id={"ctx": target},
            device_id_type=MESH,
        )

    loads = [
        pltpu.make_async_copy(src, dst, load_sem.at[i])
        for i, (src, dst) in enumerate(
            (
                (rope_hbm, rope),
                (k_hbm, k_in),
                (k_gain_hbm, k_gain),
                (q_hbm, q_in),
                (q_gain_hbm, q_gain),
                (v_hbm, vbuf.at[2]),
                (flags_hbm, flags.at[2]),
            )
        )
    ]
    for copy in loads:
        copy.start()
    load_r, load_k, load_kg, load_q, load_qg, load_v, load_f = loads

    def own(kind, first, rows):
        return (v_hbm if kind == "v" else kbuf.at[2]).at[pl.ds(first, rows)]

    def slot(kind, index, first, rows):
        return (vbuf if kind == "v" else kbuf).at[index, pl.ds(first, rows)]

    to_near, to_partner, forward = [], [], []
    for i, piece in enumerate(PIECES):
        to_near.append(remote(own(*piece), slot(piece[0], 0, *piece[1:]), i_send.at[i], i_recv.at[i], near))
        there = slot(piece[0], 1, *piece[1:])
        to_partner.append(remote(own(*piece), there, d_send.at[i], d_recv.at[i], partner))
        forward.append(
            remote(slot(piece[0], 0, *piece[1:]), there, d_send.at[i], d_recv.at[i], partner)
        )
    flags_near = remote(flags_hbm, flags.at[0], fsend_sem.at[0], frecv_sem.at[0], near)
    flags_partner = remote(flags_hbm, flags.at[1], fsend_sem.at[1], frecv_sem.at[1], partner)
    flags_forward = remote(flags.at[0], flags.at[1], fsend_sem.at[1], frecv_sem.at[1], partner)

    pl.when(has_after)(lambda: pl.semaphore_wait(barrier, 2))
    pl.when(jnp.logical_not(has_after))(lambda: pl.semaphore_wait(barrier, 1))

    def start_all(condition, copies):
        @pl.when(condition)
        def _():
            for copy in copies:
                copy.start()

    start_all(has_after, [flags_near])
    start_all(has_after & odd, to_near[:1])
    start_all(even, [flags_partner] + [to_partner[i] for i in (0, 3, 4, 5)])

    load_r.wait()
    base = (me * ROWS).astype(jnp.float32) * rope[2, :8]
    base_cos, base_sin = jnp.cos(base)[:1], jnp.sin(base)[:1]
    row_cos, row_sin = rope[0], rope[1]
    rope[0] = base_cos * row_cos - base_sin * row_sin
    rope[1] = base_sin * row_cos + base_cos * row_sin

    def normed(raw, gain, rows, scale):
        x = raw.astype(jnp.float32)
        mean = jnp.sum(x * x, axis=-1, keepdims=True) * (1.0 / HEAD)
        x = x * lax.rsqrt(mean + 1e-06) * gain
        a, b = x[:, :HALF], x[:, HALF:]
        cosine, sine = rope[0, rows], rope[1, rows]
        first = (a * cosine - b * sine).astype(jnp.bfloat16)
        second = (b * cosine + a * sine).astype(jnp.bfloat16)
        if scale != 1.0:
            first, second = first * jnp.bfloat16(scale), second * jnp.bfloat16(scale)
        return first, second

    load_k.wait()
    load_kg.wait()
    for i in (1, 2):
        rows = pl.ds(*PIECES[i][1:])
        for h in range(KEY_VALUE_HEADS):
            first, second = normed(k_in[rows, h * HEAD : (h + 1) * HEAD], k_gain[...], rows, 1.0)
            kbuf[2, rows, h * HEAD : h * HEAD + HALF] = first
            kbuf[2, rows, h * HEAD + HALF : (h + 1) * HEAD] = second
        start_all(has_after & odd, to_near[i : i + 1])
        start_all(even, to_partner[i : i + 1])
    start_all(has_after & odd, to_near[3:])

    load_q.wait()
    load_qg.wait()

    def prepare(h, carry):
        for j in range(2):
            for u in range(2):
                rows = pl.ds(u * SUB, SUB)
                raw = q_in[rows, span(h * 2 + j, HEAD)]
                first, second = normed(raw, q_gain[...], rows, HEAD**-0.5)
                qbuf[h, j, rows, :HALF] = first
                qbuf[h, j, rows, HALF:] = second
        return carry

    lax.fori_loop(0, KEY_VALUE_HEADS, prepare, 0)

    load_f.wait()

    @pl.when(has_before)
    def _():
        flags_near.wait_recv()

    start_all(forwards, [flags_forward])

    @pl.when(has_last)
    def _():
        flags_partner.wait_recv()

    @pl.when(jnp.logical_not(has_before))
    def _():
        flags[0] = jnp.zeros((1, ROWS), jnp.int32)

    @pl.when(jnp.logical_not(has_last))
    def _():
        flags[1] = jnp.zeros((1, ROWS), jnp.int32)

    first_tick = (me - 2) * ROWS
    column = lax.broadcasted_iota(jnp.int32, (1, ROWS), 1)

    def marks(index):
        place = column + index * ROWS
        return jnp.where((flags[index] == 1) & (place + first_tick >= 0), place, -first_tick)

    behind = jnp.max(jnp.maximum(marks(0), marks(1)), axis=1, keepdims=True)
    row = lax.broadcasted_iota(jnp.int32, (ROWS, ROWS), 0)
    col = lax.broadcasted_iota(jnp.int32, (ROWS, ROWS), 1)
    seen = jnp.where(col <= row, jnp.broadcast_to(marks(2), (ROWS, ROWS)), -first_tick)
    start = jnp.maximum(jnp.max(seen, axis=1, keepdims=True), behind)
    tick = lax.broadcasted_iota(jnp.int32, (ROWS, 1), 0) + WINDOW
    low[...] = jnp.broadcast_to(jnp.maximum(start, tick - (WINDOW - 1)), (ROWS, 128))

    def weigh(h, u, index, first, keys):
        ticks = pl.ds(u * SUB, SUB)
        q = qbuf[h, :, ticks, :].reshape(2 * SUB, HEAD)
        k = kbuf[index, pl.ds(first, keys), span(h, HEAD)]
        score = lax.dot_general(q, k, (((1,), (1,)), ((), ())), preferred_element_type=jnp.float32)
        offset = index * ROWS + first
        place = lax.broadcasted_iota(jnp.int32, (SUB, keys), 1) + offset
        allowed = place >= low[ticks][:, :1]
        if index == 2 and first + keys > u * SUB:
            tick = lax.broadcasted_iota(jnp.int32, (SUB, keys), 0) + (WINDOW + u * SUB)
            allowed = allowed & (place <= tick)
        weight = jnp.where(allowed[None], jnp.exp(score).reshape(2, SUB, keys), 0.0)
        weight = weight.reshape(2 * SUB, keys)
        lanes = weight[:, :128]
        for i in range(1, keys // 128):
            lanes = lanes + weight[:, i * 128 : (i + 1) * 128]
        return weight.astype(jnp.bfloat16), lanes.reshape(2, SUB, 128)

    def mix(weight, h, index, first, keys):
        v = vbuf[index, pl.ds(first, keys), span(h, HEAD)]
        mixed = jnp.dot(weight, v, preferred_element_type=jnp.float32)
        return mixed.reshape(2, weight.shape[0] // 2, HEAD)

    def part(h, u, index, first, keys, first_use=False):
        weight, lanes = weigh(h, u, index, first, keys)
        mixed = mix(weight, h, index, first, keys)
        if first_use:
            acc[h, u] = mixed
            total[h, u] = lanes
        else:
            acc[h, u] += mixed
            total[h, u] += lanes

    def each_head(step):
        lax.fori_loop(0, KEY_VALUE_HEADS, lambda h, carry: (step(h), carry)[1], 0)

    load_v.wait()

    def own_part(h):
        part(h, 0, 2, 0, SUB, True)
        part(h, 1, 2, 0, ROWS, True)

    each_head(own_part)
    start_all(has_after & even, to_near)

    def receive(pieces):
        @pl.when(forwards)
        def _():
            for i in pieces:
                to_near[i].wait_recv()
                forward[i].start()

        @pl.when(has_last)
        def _():
            for i in pieces:
                to_partner[i].wait_recv()

    def receive_own(pieces):
        @pl.when(has_before & even)
        def _():
            for i in pieces:
                to_near[i].wait_recv()

    receive((0, 1))

    @pl.when(has_last)
    def _():
        def step(h):
            part(h, 0, 1, SUB, SUB)
            part(h, 1, 1, SUB, SUB)

        each_head(step)

    receive_own((0, 1))

    @pl.when(has_before)
    def _():
        def step(h):
            part(h, 0, 0, SUB, SUB)
            part(h, 1, 0, SUB, SUB)

        each_head(step)

    receive((2,))

    @pl.when(has_last)
    def _():
        def step(h):
            for u in range(2):
                weight, lanes = weigh(h, u, 1, 0, SUB)
                held1[h, u] = weight
                total[h, u] += lanes

        each_head(step)

    receive_own((2,))

    @pl.when(has_before)
    def _():
        def step(h):
            weight, lanes = weigh(h, 0, 0, 0, SUB)
            held0[h] = weight.reshape(2, SUB, SUB)
            total[h, 0] += lanes

        each_head(step)


    def divide(h):
        for u in range(2):
            for j in range(2):
                whole = jnp.sum(total[h, u, j], axis=-1, keepdims=True)
                share = 1.0 / whole
                total[h, u, j] = jnp.broadcast_to(share, (SUB, 128))

    each_head(divide)

    def finish(h, u, first, rows, mixed):
        ticks = pl.ds(first, rows)
        for j in range(2):
            share = total[h, u, j, ticks]
            for half in range(2):
                lanes = slice(half * HALF, (half + 1) * HALF)
                value = acc[h, u, j, ticks, lanes]
                if mixed is not None:
                    value = value + mixed[j, :, lanes]
                out = pl.ds(pl.multiple_of((h * 2 + j) * HEAD + half * HALF, HALF), HALF)
                o_ref[pl.ds(u * SUB + first, rows), out] = (value * share).astype(jnp.bfloat16)

    @pl.when(has_last)
    def _():
        for i in (3, 4, 5):
            to_partner[i].wait_recv()

        def step(h):
            acc[h, 0] += mix(held1[h, 0], h, 1, 0, SUB)
            finish(h, 1, 0, SUB, mix(held1[h, 1], h, 1, 0, SUB))

        each_head(step)

    @pl.when(jnp.logical_not(has_last))
    def _():
        each_head(lambda h: finish(h, 1, 0, SUB, None))

    @pl.when(jnp.logical_not(has_before))
    def _():
        each_head(lambda h: finish(h, 0, 0, SUB, None))

    @pl.when(has_before)
    def _():
        for i in (3, 4, 5):
            first, rows = PIECES[i][1:]
            to_near[i].wait_recv()
            pl.when(odd)(forward[i].start)
            for h in range(KEY_VALUE_HEADS):
                weight = held0[h, :, pl.ds(0, first + rows), pl.ds(first, rows)]
                mixed = mix(weight.reshape(2 * (first + rows), rows), h, 0, first, rows)
                if first:
                    acc[h, 0, :, pl.ds(0, first)] += mixed[:, :first]
                finish(h, 0, first, rows, mixed[:, first:])

    @pl.when(has_after)
    def _():
        for copy in [flags_near] + to_near:
            copy.wait_send()

    @pl.when(sends_partner)
    def _():
        for copy in [flags_partner] + to_partner:
            copy.wait_send()


def solution(mesh):
    count = mesh.shape["ctx"]
    inverse = 10000.0 ** (-(np.arange(HALF, dtype=np.float64) * (2.0 / HEAD)))
    angle = np.arange(ROWS, dtype=np.float64)[:, None] * inverse
    table = np.stack([np.cos(angle), np.sin(angle), 0 * angle + inverse]).astype(np.float32)

    def body(queries, keys, values, query_gain, key_gain, session_flags, valid_length):
        assert queries.shape[0] == ROWS and 2 * ROWS == WINDOW
        pinned = functools.partial(pltpu.with_memory_space_constraint, memory_space=pltpu.HBM)
        bf16, f32, i32 = jnp.bfloat16, jnp.float32, jnp.int32
        dma = pltpu.SemaphoreType.DMA
        heads, pieces = KEY_VALUE_HEADS, len(PIECES)
        mixed = pl.pallas_call(
            functools.partial(kernel, count),
            out_shape=pltpu.VMEM((ROWS, QUERY_HEADS * HEAD), bf16),
            in_specs=[pl.BlockSpec(memory_space=pltpu.HBM)] * 7,
            out_specs=pl.BlockSpec(memory_space=pltpu.VMEM),
            scratch_shapes=[
                pltpu.VMEM((ROWS, QUERY_HEADS * HEAD), bf16),
                pltpu.VMEM((ROWS, KEY_VALUE_HEADS * HEAD), bf16),
                pltpu.VMEM((3, ROWS, HALF), f32),
                pltpu.VMEM((1, HEAD), f32),
                pltpu.VMEM((1, HEAD), f32),
                pltpu.VMEM((3, ROWS, KEY_VALUE_HEADS * HEAD), bf16),
                pltpu.VMEM((3, ROWS, KEY_VALUE_HEADS * HEAD), bf16),
                pltpu.VMEM((heads, 2, ROWS, HEAD), bf16),
                pltpu.VMEM((3, 1, ROWS), i32),
                pltpu.VMEM((ROWS, 128), i32),
                pltpu.VMEM((heads, 2, 2, SUB, HEAD), f32),
                pltpu.VMEM((heads, 2, 2, SUB, 128), f32),
                pltpu.VMEM((heads, 2, SUB, SUB), bf16),
                pltpu.VMEM((heads, 2, 2 * SUB, SUB), bf16),
                dma((7,)),
                dma((2,)),
                dma((2,)),
                dma((pieces,)),
                dma((pieces,)),
                dma((pieces,)),
                dma((pieces,)),
            ],
            compiler_params=pltpu.CompilerParams(
                collective_id=0, has_side_effects=True, vmem_limit_bytes=56 << 20
            ),
        )(
            pinned(queries),
            pinned(keys),
            pinned(values),
            pinned(query_gain.reshape(1, HEAD)),
            pinned(key_gain.reshape(1, HEAD)),
            pinned(session_flags.reshape(1, ROWS)),
            pinned(jnp.asarray(table)),
        )

        first = (count - 1) * ROWS

        def cut(mixed, limit):
            tick = first + lax.broadcasted_iota(i32, mixed.shape, 0)
            return jnp.where(tick < limit[0], mixed, jnp.zeros((), bf16))

        return lax.cond(
            lax.axis_index("ctx") == count - 1, cut, lambda mixed, limit: mixed, mixed, valid_length
        )

    return jax.shard_map(
        body,
        mesh=mesh,
        in_specs=(
            P(("dates", "ctx"), None),
            P(("dates", "ctx"), None),
            P(("dates", "ctx"), None),
            P(),
            P(),
            P(("dates", "ctx")),
            P("dates"),
        ),
        out_specs=P(("dates", "ctx"), None),
        check_vma=False,
    )
```

```python
import functools

import jax
import jax.numpy as jnp
import numpy as np
from jax import lax
from jax.experimental import pallas as pl
from jax.experimental.pallas import tpu as pltpu
from jax.sharding import PartitionSpec as P

QUERY_HEADS = 8
KEY_VALUE_HEADS = 4
HEAD = 256
HALF = HEAD // 2
WINDOW = 1024
ROWS = 512
SUB = 256
MESH = pl.DeviceIdType.MESH

PIECES = (
    ("v", 304, 208),
    ("k", 256, 256),
    ("k", 0, 256),
    ("v", 128, 128),
    ("v", 64, 64),
    ("v", 0, 64),
    ("v", 256, 48),
)
UNIT = 6
FIRST, LAST = (0, UNIT, 1), (3, 4, 5)
AROUND = (1, 3, 5)


def kernel(
    count,
    q_hbm,
    k_hbm,
    v_hbm,
    q_gain_hbm,
    k_gain_hbm,
    flags_hbm,
    rope_hbm,
    o_ref,
    q_in,
    k_in,
    rope,
    q_gain,
    k_gain,
    kbuf,
    vbuf,
    qbuf,
    flags,
    low,
    acc,
    total,
    held0,
    held1,
    relay,
    load_sem,
    fsend_sem,
    frecv_sem,
    i_send,
    i_recv,
    d_send,
    d_recv,
    r_send,
    r_recv,
):
    me = lax.axis_index("ctx")
    core = lax.rem(me, 2)
    even, odd = core == 0, core == 1
    chip = me // 2
    chips = count // 2
    near = lax.rem(me + 2, count)
    back = lax.rem(me + count - 2, count)
    partner = me + 1 - 2 * core
    has_after, has_before = chip < chips - 1, chip > 0
    forwards = odd & has_before
    sends_partner = even | has_before
    has_last = me > 0

    barrier = pltpu.get_barrier_semaphore()

    def ready(target):
        pl.semaphore_signal(barrier, inc=1, device_id={"ctx": target}, device_id_type=MESH)

    hub = me == 0
    around = [c for c in AROUND if c + 1 < chips]
    goes_around = functools.reduce(jnp.logical_or, [me == 2 * c for c in around], me < 0)

    pl.when(has_before)(lambda: ready(back))
    ready(partner)
    for c in around:
        pl.when(hub)(functools.partial(ready, 2 * c))
        pl.when(me == 2 * c + 2)(functools.partial(ready, 0))

    def span(index, width):
        return pl.ds(pl.multiple_of(index * width, width), width)

    def remote(src, dst, send, recv, target):
        return pltpu.make_async_remote_copy(
            src_ref=src,
            dst_ref=dst,
            send_sem=send,
            recv_sem=recv,
            device_id={"ctx": target},
            device_id_type=MESH,
        )

    loads = [
        pltpu.make_async_copy(src, dst, load_sem.at[i])
        for i, (src, dst) in enumerate(
            (
                (rope_hbm, rope),
                (k_hbm, k_in),
                (k_gain_hbm, k_gain),
                (q_hbm, q_in),
                (q_gain_hbm, q_gain),
                (v_hbm, vbuf.at[2]),
                (flags_hbm, flags.at[2]),
            )
        )
    ]
    for copy in loads:
        copy.start()
    load_r, load_k, load_kg, load_q, load_qg, load_v, load_f = loads

    def own(kind, first, rows):
        return (v_hbm if kind == "v" else kbuf.at[2]).at[pl.ds(first, rows)]

    def slot(kind, index, first, rows):
        return (vbuf if kind == "v" else kbuf).at[index, pl.ds(first, rows)]

    to_near, to_partner, forward = [], [], []
    for i, piece in enumerate(PIECES):
        to_near.append(remote(own(*piece), slot(piece[0], 0, *piece[1:]), i_send.at[i], i_recv.at[i], near))
        there = slot(piece[0], 1, *piece[1:])
        to_partner.append(remote(own(*piece), there, d_send.at[i], d_recv.at[i], partner))
        forward.append(
            remote(slot(piece[0], 0, *piece[1:]), there, d_send.at[i], d_recv.at[i], partner)
        )
    flags_near = remote(flags_hbm, flags.at[0], fsend_sem.at[0], frecv_sem.at[0], near)
    flags_partner = remote(flags_hbm, flags.at[1], fsend_sem.at[1], frecv_sem.at[1], partner)
    flags_forward = remote(flags.at[0], flags.at[1], fsend_sem.at[1], frecv_sem.at[1], partner)

    there = slot("v", 0, *PIECES[UNIT][1:])
    to_hub, onward = [], []
    for r, c in enumerate(around):
        to_hub.append(remote(own(*PIECES[UNIT]), relay.at[r], i_send.at[UNIT], r_recv.at[r], 0))
        onward.append(remote(relay.at[r], there, r_send.at[r], i_recv.at[UNIT], 2 * c + 2))

    greetings = 1 + has_after.astype(jnp.int32) + goes_around.astype(jnp.int32)
    pl.semaphore_wait(barrier, greetings + len(around) * hub.astype(jnp.int32))

    def start_all(condition, copies):
        @pl.when(condition)
        def _():
            for copy in copies:
                copy.start()

    start_all(has_after, [flags_near])
    start_all(has_after & odd, [to_near[i] for i in (0, UNIT)])
    for c, copy in zip(around, to_hub):
        start_all(me == 2 * c, [copy])
    start_all(even, [flags_partner] + [to_partner[i] for i in (0, UNIT) + LAST])

    load_r.wait()
    base = (me * ROWS).astype(jnp.float32) * rope[2, :8]
    base_cos, base_sin = jnp.cos(base)[:1], jnp.sin(base)[:1]
    row_cos, row_sin = rope[0], rope[1]
    rope[0] = base_cos * row_cos - base_sin * row_sin
    rope[1] = base_sin * row_cos + base_cos * row_sin

    def normed(raw, gain, rows, scale):
        x = raw.astype(jnp.float32)
        mean = jnp.sum(x * x, axis=-1, keepdims=True) * (1.0 / HEAD)
        x = x * lax.rsqrt(mean + 1e-06) * gain
        a, b = x[:, :HALF], x[:, HALF:]
        cosine, sine = rope[0, rows], rope[1, rows]
        first = (a * cosine - b * sine).astype(jnp.bfloat16)
        second = (b * cosine + a * sine).astype(jnp.bfloat16)
        if scale != 1.0:
            first, second = first * jnp.bfloat16(scale), second * jnp.bfloat16(scale)
        return first, second

    load_k.wait()
    load_kg.wait()
    for i in (1, 2):
        rows = pl.ds(*PIECES[i][1:])
        for h in range(KEY_VALUE_HEADS):
            first, second = normed(k_in[rows, h * HEAD : (h + 1) * HEAD], k_gain[...], rows, 1.0)
            kbuf[2, rows, h * HEAD : h * HEAD + HALF] = first
            kbuf[2, rows, h * HEAD + HALF : (h + 1) * HEAD] = second
        start_all(has_after & odd, to_near[i : i + 1])
        start_all(even, to_partner[i : i + 1])
    start_all(has_after & odd, [to_near[i] for i in LAST])

    load_q.wait()
    load_qg.wait()

    def prepare(h, carry):
        for j in range(2):
            for u in range(2):
                rows = pl.ds(u * SUB, SUB)
                raw = q_in[rows, span(h * 2 + j, HEAD)]
                first, second = normed(raw, q_gain[...], rows, HEAD**-0.5)
                qbuf[h, j, rows, :HALF] = first
                qbuf[h, j, rows, HALF:] = second
        return carry

    lax.fori_loop(0, KEY_VALUE_HEADS, prepare, 0)

    load_f.wait()

    @pl.when(has_before)
    def _():
        flags_near.wait_recv()

    start_all(forwards, [flags_forward])

    @pl.when(has_last)
    def _():
        flags_partner.wait_recv()

    @pl.when(jnp.logical_not(has_before))
    def _():
        flags[0] = jnp.zeros((1, ROWS), jnp.int32)

    @pl.when(jnp.logical_not(has_last))
    def _():
        flags[1] = jnp.zeros((1, ROWS), jnp.int32)

    first_tick = (me - 2) * ROWS
    column = lax.broadcasted_iota(jnp.int32, (1, ROWS), 1)

    def marks(index):
        place = column + index * ROWS
        return jnp.where((flags[index] == 1) & (place + first_tick >= 0), place, -first_tick)

    behind = jnp.max(jnp.maximum(marks(0), marks(1)), axis=1, keepdims=True)
    row = lax.broadcasted_iota(jnp.int32, (ROWS, ROWS), 0)
    col = lax.broadcasted_iota(jnp.int32, (ROWS, ROWS), 1)
    seen = jnp.where(col <= row, jnp.broadcast_to(marks(2), (ROWS, ROWS)), -first_tick)
    start = jnp.maximum(jnp.max(seen, axis=1, keepdims=True), behind)
    tick = lax.broadcasted_iota(jnp.int32, (ROWS, 1), 0) + WINDOW
    low[...] = jnp.broadcast_to(jnp.maximum(start, tick - (WINDOW - 1)), (ROWS, 128))

    def weigh(h, u, index, first, keys):
        ticks = pl.ds(u * SUB, SUB)
        q = qbuf[h, :, ticks, :].reshape(2 * SUB, HEAD)
        k = kbuf[index, pl.ds(first, keys), span(h, HEAD)]
        score = lax.dot_general(q, k, (((1,), (1,)), ((), ())), preferred_element_type=jnp.float32)
        offset = index * ROWS + first
        place = lax.broadcasted_iota(jnp.int32, (SUB, keys), 1) + offset
        allowed = place >= low[ticks][:, :1]
        if index == 2 and first + keys > u * SUB:
            tick = lax.broadcasted_iota(jnp.int32, (SUB, keys), 0) + (WINDOW + u * SUB)
            allowed = allowed & (place <= tick)
        weight = jnp.where(allowed[None], jnp.exp(score).reshape(2, SUB, keys), 0.0)
        weight = weight.reshape(2 * SUB, keys)
        lanes = weight[:, :128]
        for i in range(1, keys // 128):
            lanes = lanes + weight[:, i * 128 : (i + 1) * 128]
        return weight.astype(jnp.bfloat16), lanes.reshape(2, SUB, 128)

    def mix(weight, h, index, first, keys):
        v = vbuf[index, pl.ds(first, keys), span(h, HEAD)]
        mixed = jnp.dot(weight, v, preferred_element_type=jnp.float32)
        return mixed.reshape(2, weight.shape[0] // 2, HEAD)

    def part(h, u, index, first, keys, first_use=False):
        weight, lanes = weigh(h, u, index, first, keys)
        mixed = mix(weight, h, index, first, keys)
        if first_use:
            acc[h, u] = mixed
            total[h, u] = lanes
        else:
            acc[h, u] += mixed
            total[h, u] += lanes

    def each_head(step):
        lax.fori_loop(0, KEY_VALUE_HEADS, lambda h, carry: (step(h), carry)[1], 0)

    load_v.wait()

    def own_part(h):
        part(h, 0, 2, 0, SUB, True)
        part(h, 1, 2, 0, ROWS, True)

    each_head(own_part)

    @pl.when(hub)
    def _():
        for came, goes in zip(to_hub, onward):
            came.wait_recv()
            goes.start()

    start_all(has_after & even & jnp.logical_not(goes_around), [to_near[UNIT]])
    start_all(has_after & even, to_near[:UNIT])

    def receive(pieces):
        @pl.when(forwards)
        def _():
            for i in pieces:
                to_near[i].wait_recv()
                forward[i].start()

        @pl.when(has_last)
        def _():
            for i in pieces:
                to_partner[i].wait_recv()

    def receive_own(pieces):
        @pl.when(has_before & even)
        def _():
            for i in pieces:
                to_near[i].wait_recv()

    receive(FIRST)

    @pl.when(has_last)
    def _():
        def step(h):
            part(h, 0, 1, SUB, SUB)
            part(h, 1, 1, SUB, SUB)

        each_head(step)

    receive_own(FIRST)

    @pl.when(has_before)
    def _():
        def step(h):
            part(h, 0, 0, SUB, SUB)
            part(h, 1, 0, SUB, SUB)

        each_head(step)

    receive((2,))

    @pl.when(has_last)
    def _():
        def step(h):
            for u in range(2):
                weight, lanes = weigh(h, u, 1, 0, SUB)
                held1[h, u] = weight
                total[h, u] += lanes

        each_head(step)

    receive_own((2,))

    @pl.when(has_before)
    def _():
        def step(h):
            weight, lanes = weigh(h, 0, 0, 0, SUB)
            held0[h] = weight.reshape(2, SUB, SUB)
            total[h, 0] += lanes

        each_head(step)


    def divide(h):
        for u in range(2):
            for j in range(2):
                whole = jnp.sum(total[h, u, j], axis=-1, keepdims=True)
                share = 1.0 / whole
                total[h, u, j] = jnp.broadcast_to(share, (SUB, 128))

    each_head(divide)

    def finish(h, u, first, rows, mixed):
        ticks = pl.ds(first, rows)
        for j in range(2):
            share = total[h, u, j, ticks]
            for half in range(2):
                lanes = slice(half * HALF, (half + 1) * HALF)
                value = acc[h, u, j, ticks, lanes]
                if mixed is not None:
                    value = value + mixed[j, :, lanes]
                out = pl.ds(pl.multiple_of((h * 2 + j) * HEAD + half * HALF, HALF), HALF)
                o_ref[pl.ds(u * SUB + first, rows), out] = (value * share).astype(jnp.bfloat16)

    @pl.when(has_last)
    def _():
        for i in LAST:
            to_partner[i].wait_recv()

        def step(h):
            acc[h, 0] += mix(held1[h, 0], h, 1, 0, SUB)
            finish(h, 1, 0, SUB, mix(held1[h, 1], h, 1, 0, SUB))

        each_head(step)

    @pl.when(jnp.logical_not(has_last))
    def _():
        each_head(lambda h: finish(h, 1, 0, SUB, None))

    @pl.when(jnp.logical_not(has_before))
    def _():
        each_head(lambda h: finish(h, 0, 0, SUB, None))

    @pl.when(has_before)
    def _():
        for i in LAST:
            first, rows = PIECES[i][1:]
            to_near[i].wait_recv()
            pl.when(odd)(forward[i].start)
            for h in range(KEY_VALUE_HEADS):
                weight = held0[h, :, pl.ds(0, first + rows), pl.ds(first, rows)]
                mixed = mix(weight.reshape(2 * (first + rows), rows), h, 0, first, rows)
                if first:
                    acc[h, 0, :, pl.ds(0, first)] += mixed[:, :first]
                finish(h, 0, first, rows, mixed[:, first:])

    @pl.when(has_after)
    def _():
        for copy in [flags_near] + to_near:
            copy.wait_send()

    @pl.when(sends_partner)
    def _():
        for copy in [flags_partner] + to_partner:
            copy.wait_send()

    @pl.when(hub)
    def _():
        for copy in onward:
            copy.wait_send()


def solution(mesh):
    count = mesh.shape["ctx"]
    inverse = 10000.0 ** (-(np.arange(HALF, dtype=np.float64) * (2.0 / HEAD)))
    angle = np.arange(ROWS, dtype=np.float64)[:, None] * inverse
    table = np.stack([np.cos(angle), np.sin(angle), 0 * angle + inverse]).astype(np.float32)

    def body(queries, keys, values, query_gain, key_gain, session_flags, valid_length):
        assert queries.shape[0] == ROWS and 2 * ROWS == WINDOW
        pinned = functools.partial(pltpu.with_memory_space_constraint, memory_space=pltpu.HBM)
        bf16, f32, i32 = jnp.bfloat16, jnp.float32, jnp.int32
        dma = pltpu.SemaphoreType.DMA
        heads, pieces = KEY_VALUE_HEADS, len(PIECES)
        mixed = pl.pallas_call(
            functools.partial(kernel, count),
            out_shape=pltpu.VMEM((ROWS, QUERY_HEADS * HEAD), bf16),
            in_specs=[pl.BlockSpec(memory_space=pltpu.HBM)] * 7,
            out_specs=pl.BlockSpec(memory_space=pltpu.VMEM),
            scratch_shapes=[
                pltpu.VMEM((ROWS, QUERY_HEADS * HEAD), bf16),
                pltpu.VMEM((ROWS, KEY_VALUE_HEADS * HEAD), bf16),
                pltpu.VMEM((3, ROWS, HALF), f32),
                pltpu.VMEM((1, HEAD), f32),
                pltpu.VMEM((1, HEAD), f32),
                pltpu.VMEM((3, ROWS, KEY_VALUE_HEADS * HEAD), bf16),
                pltpu.VMEM((3, ROWS, KEY_VALUE_HEADS * HEAD), bf16),
                pltpu.VMEM((heads, 2, ROWS, HEAD), bf16),
                pltpu.VMEM((3, 1, ROWS), i32),
                pltpu.VMEM((ROWS, 128), i32),
                pltpu.VMEM((heads, 2, 2, SUB, HEAD), f32),
                pltpu.VMEM((heads, 2, 2, SUB, 128), f32),
                pltpu.VMEM((heads, 2, SUB, SUB), bf16),
                pltpu.VMEM((heads, 2, 2 * SUB, SUB), bf16),
                pltpu.VMEM((len(AROUND), PIECES[UNIT][2], heads * HEAD), bf16),
                dma((7,)),
                dma((2,)),
                dma((2,)),
                dma((pieces,)),
                dma((pieces,)),
                dma((pieces,)),
                dma((pieces,)),
                dma((len(AROUND),)),
                dma((len(AROUND),)),
            ],
            compiler_params=pltpu.CompilerParams(
                collective_id=0, has_side_effects=True, vmem_limit_bytes=56 << 20
            ),
        )(
            pinned(queries),
            pinned(keys),
            pinned(values),
            pinned(query_gain.reshape(1, HEAD)),
            pinned(key_gain.reshape(1, HEAD)),
            pinned(session_flags.reshape(1, ROWS)),
            pinned(jnp.asarray(table)),
        )

        first = (count - 1) * ROWS

        def cut(mixed, limit):
            tick = first + lax.broadcasted_iota(i32, mixed.shape, 0)
            return jnp.where(tick < limit[0], mixed, jnp.zeros((), bf16))

        return lax.cond(
            lax.axis_index("ctx") == count - 1, cut, lambda mixed, limit: mixed, mixed, valid_length
        )

    return jax.shard_map(
        body,
        mesh=mesh,
        in_specs=(
            P(("dates", "ctx"), None),
            P(("dates", "ctx"), None),
            P(("dates", "ctx"), None),
            P(),
            P(),
            P(("dates", "ctx")),
            P("dates"),
        ),
        out_specs=P(("dates", "ctx"), None),
        check_vma=False,
    )
```

```python
import functools

import jax
import jax.numpy as jnp
import numpy as np
from jax import lax
from jax.experimental import pallas as pl
from jax.experimental.pallas import tpu as pltpu
from jax.sharding import PartitionSpec as P

QUERY_HEADS = 8
KEY_VALUE_HEADS = 4
HEAD = 256
HALF = HEAD // 2
WINDOW = 1024
ROWS = 512
SUB = 256
MESH = pl.DeviceIdType.MESH

PIECES = (
    ("v", 336, 176),
    ("k", 256, 256),
    ("k", 0, 256),
    ("v", 128, 128),
    ("v", 64, 64),
    ("v", 0, 64),
    ("v", 256, 80),
)
UNIT, WEIGHTS = 6, 7
EDGE_ROWS = 32
PACK = 128 // EDGE_ROWS
FIRST, LAST = (0, UNIT, 1), (3, 4, 5)
AROUND = (1, 3, 5)
TAKERS = (1, 3, 5, 7)


def kernel(
    count,
    q_hbm,
    k_hbm,
    v_hbm,
    q_gain_hbm,
    k_gain_hbm,
    flags_hbm,
    rope_hbm,
    o_ref,
    q_in,
    k_in,
    rope,
    q_gain,
    k_gain,
    kbuf,
    vbuf,
    qbuf,
    flags,
    low,
    acc,
    total,
    held0,
    held1,
    relay,
    q_edge,
    q_relay,
    w_out,
    w_in,
    load_sem,
    fsend_sem,
    frecv_sem,
    i_send,
    i_recv,
    d_send,
    d_recv,
    r_send,
    r_recv,
    q_send,
    q_recv,
):
    me = lax.axis_index("ctx")
    core = lax.rem(me, 2)
    even, odd = core == 0, core == 1
    chip = me // 2
    chips = count // 2
    near = lax.rem(me + 2, count)
    back = lax.rem(me + count - 2, count)
    partner = me + 1 - 2 * core
    has_after, has_before = chip < chips - 1, chip > 0
    forwards = odd & has_before
    sends_partner = even | has_before
    has_last = me > 0

    barrier = pltpu.get_barrier_semaphore()

    def ready(target):
        pl.semaphore_signal(barrier, inc=1, device_id={"ctx": target}, device_id_type=MESH)

    hub = me == 0
    around = [c for c in AROUND if c + 1 < chips]
    takers = [c for c in TAKERS if c < chips]

    def one_of(devices):
        return functools.reduce(jnp.logical_or, [me == d for d in devices], me < 0)

    goes_around = one_of([2 * c for c in around])
    takes_edge = one_of([2 * c for c in takers])
    gives_edge = one_of([2 * c - 2 for c in takers])

    pl.when(has_before)(lambda: ready(back))
    ready(partner)
    for c in takers:
        pl.when(hub)(functools.partial(ready, 2 * c))
    for c in around:
        pl.when(me == 2 * c + 2)(functools.partial(ready, 0))

    def span(index, width):
        return pl.ds(pl.multiple_of(index * width, width), width)

    def remote(src, dst, send, recv, target):
        return pltpu.make_async_remote_copy(
            src_ref=src,
            dst_ref=dst,
            send_sem=send,
            recv_sem=recv,
            device_id={"ctx": target},
            device_id_type=MESH,
        )

    loads = [
        pltpu.make_async_copy(src, dst, load_sem.at[i])
        for i, (src, dst) in enumerate(
            (
                (rope_hbm, rope),
                (k_hbm, k_in),
                (k_gain_hbm, k_gain),
                (q_hbm, q_in),
                (q_gain_hbm, q_gain),
                (v_hbm, vbuf.at[2]),
                (flags_hbm, flags.at[2]),
            )
        )
    ]
    for copy in loads:
        copy.start()
    load_r, load_k, load_kg, load_q, load_qg, load_v, load_f = loads

    def own(kind, first, rows):
        return (v_hbm if kind == "v" else kbuf.at[2]).at[pl.ds(first, rows)]

    def slot(kind, index, first, rows):
        return (vbuf if kind == "v" else kbuf).at[index, pl.ds(first, rows)]

    to_near, to_partner, forward = [], [], []
    for i, piece in enumerate(PIECES):
        to_near.append(remote(own(*piece), slot(piece[0], 0, *piece[1:]), i_send.at[i], i_recv.at[i], near))
        there = slot(piece[0], 1, *piece[1:])
        to_partner.append(remote(own(*piece), there, d_send.at[i], d_recv.at[i], partner))
        forward.append(
            remote(slot(piece[0], 0, *piece[1:]), there, d_send.at[i], d_recv.at[i], partner)
        )
    flags_near = remote(flags_hbm, flags.at[0], fsend_sem.at[0], frecv_sem.at[0], near)
    flags_partner = remote(flags_hbm, flags.at[1], fsend_sem.at[1], frecv_sem.at[1], partner)
    flags_forward = remote(flags.at[0], flags.at[1], fsend_sem.at[1], frecv_sem.at[1], partner)

    there = slot("v", 0, *PIECES[UNIT][1:])
    to_hub, onward = [], []
    for r, c in enumerate(around):
        to_hub.append(remote(own(*PIECES[UNIT]), relay.at[r], i_send.at[UNIT], r_recv.at[r], 0))
        onward.append(remote(relay.at[r], there, r_send.at[r], i_recv.at[UNIT], 2 * c + 2))

    q_rows = qbuf.at[:, :, pl.ds(0, EDGE_ROWS), :]
    q_to_hub, q_onward = [], []
    for r, c in enumerate(takers):
        target = q_relay.at[r] if r else q_edge
        q_to_hub.append(remote(q_rows, target, q_send.at[0], q_recv.at[r], 0))
        q_onward.append(remote(q_relay.at[r], q_edge, q_send.at[r], q_recv.at[0], 2 * c - 2))
    short = ("k", EDGE_ROWS, SUB - EDGE_ROWS)
    keys_short = remote(own(*short), slot("k", 0, *short[1:]), i_send.at[2], i_recv.at[2], near)
    weights = remote(w_out, w_in, i_send.at[WEIGHTS], i_recv.at[WEIGHTS], near)

    @pl.when(takes_edge)
    def _():
        kbuf[0, pl.ds(0, EDGE_ROWS), :] = jnp.zeros((EDGE_ROWS, KEY_VALUE_HEADS * HEAD), jnp.bfloat16)

    greetings = 1 + has_after.astype(jnp.int32) + takes_edge.astype(jnp.int32)
    pl.semaphore_wait(barrier, greetings + len(around) * hub.astype(jnp.int32))

    def start_all(condition, copies):
        @pl.when(condition)
        def _():
            for copy in copies:
                copy.start()

    start_all(has_after, [flags_near])
    start_all(has_after & odd, [to_near[i] for i in (0, UNIT)])
    for c, copy in zip(around, to_hub):
        start_all(me == 2 * c, [copy])
    start_all(even, [flags_partner] + [to_partner[i] for i in (0, UNIT) + LAST])

    load_r.wait()
    base = (me * ROWS).astype(jnp.float32) * rope[2, :8]
    base_cos, base_sin = jnp.cos(base)[:1], jnp.sin(base)[:1]
    row_cos, row_sin = rope[0], rope[1]
    rope[0] = base_cos * row_cos - base_sin * row_sin
    rope[1] = base_sin * row_cos + base_cos * row_sin

    def normed(raw, gain, rows, scale):
        x = raw.astype(jnp.float32)
        mean = jnp.sum(x * x, axis=-1, keepdims=True) * (1.0 / HEAD)
        x = x * lax.rsqrt(mean + 1e-06) * gain
        a, b = x[:, :HALF], x[:, HALF:]
        cosine, sine = rope[0, rows], rope[1, rows]
        first = (a * cosine - b * sine).astype(jnp.bfloat16)
        second = (b * cosine + a * sine).astype(jnp.bfloat16)
        if scale != 1.0:
            first, second = first * jnp.bfloat16(scale), second * jnp.bfloat16(scale)
        return first, second

    load_k.wait()
    load_kg.wait()
    for block, ready_pieces in ((SUB, (1,)), (0, (2,))):
        rows = pl.ds(block, SUB)
        for h in range(KEY_VALUE_HEADS):
            first, second = normed(k_in[rows, h * HEAD : (h + 1) * HEAD], k_gain[...], rows, 1.0)
            kbuf[2, rows, h * HEAD : h * HEAD + HALF] = first
            kbuf[2, rows, h * HEAD + HALF : (h + 1) * HEAD] = second
        start_all(has_after & odd, [to_near[i] for i in ready_pieces])
        start_all(even, [to_partner[i] for i in ready_pieces])
    start_all(has_after & odd, [to_near[i] for i in LAST])

    load_q.wait()
    load_qg.wait()

    def prepare(h, carry):
        for j in range(2):
            for u in range(2):
                rows = pl.ds(u * SUB, SUB)
                raw = q_in[rows, span(h * 2 + j, HEAD)]
                first, second = normed(raw, q_gain[...], rows, HEAD**-0.5)
                qbuf[h, j, rows, :HALF] = first
                qbuf[h, j, rows, HALF:] = second
        return carry

    lax.fori_loop(0, KEY_VALUE_HEADS, prepare, 0)
    for c, copy in zip(takers, q_to_hub):
        start_all(me == 2 * c, [copy])

    load_f.wait()

    @pl.when(has_before)
    def _():
        flags_near.wait_recv()

    start_all(forwards, [flags_forward])

    @pl.when(has_last)
    def _():
        flags_partner.wait_recv()

    @pl.when(jnp.logical_not(has_before))
    def _():
        flags[0] = jnp.zeros((1, ROWS), jnp.int32)

    @pl.when(jnp.logical_not(has_last))
    def _():
        flags[1] = jnp.zeros((1, ROWS), jnp.int32)

    first_tick = (me - 2) * ROWS
    column = lax.broadcasted_iota(jnp.int32, (1, ROWS), 1)

    def marks(index):
        place = column + index * ROWS
        return jnp.where((flags[index] == 1) & (place + first_tick >= 0), place, -first_tick)

    behind = jnp.max(jnp.maximum(marks(0), marks(1)), axis=1, keepdims=True)
    row = lax.broadcasted_iota(jnp.int32, (ROWS, ROWS), 0)
    col = lax.broadcasted_iota(jnp.int32, (ROWS, ROWS), 1)
    seen = jnp.where(col <= row, jnp.broadcast_to(marks(2), (ROWS, ROWS)), -first_tick)
    start = jnp.maximum(jnp.max(seen, axis=1, keepdims=True), behind)
    tick = lax.broadcasted_iota(jnp.int32, (ROWS, 1), 0) + WINDOW
    low[...] = jnp.broadcast_to(jnp.maximum(start, tick - (WINDOW - 1)), (ROWS, 128))

    def weigh(h, u, index, first, keys, least=None):
        ticks = pl.ds(u * SUB, SUB)
        q = qbuf[h, :, ticks, :].reshape(2 * SUB, HEAD)
        k = kbuf[index, pl.ds(first, keys), span(h, HEAD)]
        score = lax.dot_general(q, k, (((1,), (1,)), ((), ())), preferred_element_type=jnp.float32)
        offset = index * ROWS + first
        place = lax.broadcasted_iota(jnp.int32, (SUB, keys), 1) + offset
        allowed = place >= low[ticks][:, :1]
        if least is not None:
            allowed = allowed & (place >= least)
        if index == 2 and first + keys > u * SUB:
            tick = lax.broadcasted_iota(jnp.int32, (SUB, keys), 0) + (WINDOW + u * SUB)
            allowed = allowed & (place <= tick)
        weight = jnp.where(allowed[None], jnp.exp(score).reshape(2, SUB, keys), 0.0)
        weight = weight.reshape(2 * SUB, keys)
        lanes = weight[:, :128]
        for i in range(1, keys // 128):
            lanes = lanes + weight[:, i * 128 : (i + 1) * 128]
        return weight.astype(jnp.bfloat16), lanes.reshape(2, SUB, 128)

    def mix(weight, h, index, first, keys):
        v = vbuf[index, pl.ds(first, keys), span(h, HEAD)]
        mixed = jnp.dot(weight, v, preferred_element_type=jnp.float32)
        return mixed.reshape(2, weight.shape[0] // 2, HEAD)

    def part(h, u, index, first, keys, first_use=False):
        weight, lanes = weigh(h, u, index, first, keys)
        mixed = mix(weight, h, index, first, keys)
        if first_use:
            acc[h, u] = mixed
            total[h, u] = lanes
        else:
            acc[h, u] += mixed
            total[h, u] += lanes

    def each_head(step):
        lax.fori_loop(0, KEY_VALUE_HEADS, lambda h, carry: (step(h), carry)[1], 0)

    load_v.wait()

    def own_part(h):
        part(h, 0, 2, 0, SUB, True)
        part(h, 1, 2, 0, ROWS, True)

    each_head(own_part)

    @pl.when(hub)
    def _():
        for came, goes in zip(to_hub, onward):
            came.wait_recv()
            goes.start()
        for came, goes in zip(q_to_hub[1:], q_onward[1:]):
            came.wait_recv()
            goes.start()

    start_all(has_after & even & jnp.logical_not(goes_around), [to_near[UNIT]])
    start_all(has_after & even, to_near[:2])
    sends_whole = has_after & jnp.logical_not(gives_edge)
    start_all(even & sends_whole, [to_near[i] for i in (2,) + LAST])
    start_all(gives_edge, [keys_short])

    def receive(pieces):
        @pl.when(forwards)
        def _():
            for i in pieces:
                to_near[i].wait_recv()
                forward[i].start()

        @pl.when(has_last)
        def _():
            for i in pieces:
                to_partner[i].wait_recv()

    def receive_own(pieces):
        @pl.when(has_before & even)
        def _():
            for i in pieces:
                to_near[i].wait_recv()

    receive(FIRST)

    @pl.when(has_last)
    def _():
        def step(h):
            part(h, 0, 1, SUB, SUB)
            part(h, 1, 1, SUB, SUB)

        each_head(step)

    @pl.when(gives_edge)
    def _():
        q_to_hub[0].wait_recv()
        tick = lax.broadcasted_iota(jnp.int32, (EDGE_ROWS, 128), 0)
        place = lax.broadcasted_iota(jnp.int32, (EDGE_ROWS, 128), 1)
        for g in range(QUERY_HEADS // PACK):
            packed = jnp.zeros((EDGE_ROWS, 128), jnp.float32)
            for p in range(PACK):
                h, j = divmod(g * PACK + p, 2)
                k = kbuf[2, :128, h * HEAD : (h + 1) * HEAD]
                score = lax.dot_general(
                    q_edge[h, j], k, (((1,), (1,)), ((), ())), preferred_element_type=jnp.float32
                )
                weight = jnp.where((place > tick) & (place < EDGE_ROWS), jnp.exp(score), 0.0)
                packed = packed + (pltpu.roll(weight, p * EDGE_ROWS, 1) if p else weight)
            w_out[g] = packed.astype(jnp.bfloat16)
        weights.start()
        for i in LAST:
            to_near[i].start()

    receive_own(FIRST)

    @pl.when(has_before)
    def _():
        def step(h):
            part(h, 0, 0, SUB, SUB)
            part(h, 1, 0, SUB, SUB)

        each_head(step)

    receive((2,))

    @pl.when(has_last)
    def _():
        def step(h):
            for u in range(2):
                weight, lanes = weigh(h, u, 1, 0, SUB)
                held1[h, u] = weight
                total[h, u] += lanes

        each_head(step)

    pl.when(takes_edge)(keys_short.wait_recv)
    pl.when(has_before & even & jnp.logical_not(takes_edge))(to_near[2].wait_recv)

    least = jnp.where(takes_edge, EDGE_ROWS, 0)

    @pl.when(has_before)
    def _():
        def step(h):
            weight, lanes = weigh(h, 0, 0, 0, SUB, least)
            held0[h] = weight.reshape(2, SUB, SUB)
            total[h, 0] += lanes

        each_head(step)


    @pl.when(takes_edge)
    def _():
        weights.wait_recv()
        ticks = pl.ds(0, EDGE_ROWS)
        place = lax.broadcasted_iota(jnp.int32, (EDGE_ROWS, 128), 1)
        allowed = (place >= low[ticks]) & (place < EDGE_ROWS)
        for g in range(QUERY_HEADS // PACK):
            packed = w_in[g].astype(jnp.float32)
            for p in range(PACK):
                h, j = divmod(g * PACK + p, 2)
                weight = pltpu.roll(packed, 128 - p * EDGE_ROWS, 1) if p else packed
                weight = jnp.where(allowed, weight, 0.0)
                total[h, 0, j, ticks] += weight
                kept = held0[h, j, ticks, :128].astype(jnp.float32)
                held0[h, j, ticks, :128] = (kept + weight).astype(jnp.bfloat16)

    def divide(h):
        for u in range(2):
            for j in range(2):
                whole = jnp.sum(total[h, u, j], axis=-1, keepdims=True)
                share = 1.0 / whole
                total[h, u, j] = jnp.broadcast_to(share, (SUB, 128))

    each_head(divide)

    def finish(h, u, first, rows, mixed):
        ticks = pl.ds(first, rows)
        for j in range(2):
            share = total[h, u, j, ticks]
            for half in range(2):
                lanes = slice(half * HALF, (half + 1) * HALF)
                value = acc[h, u, j, ticks, lanes]
                if mixed is not None:
                    value = value + mixed[j, :, lanes]
                out = pl.ds(pl.multiple_of((h * 2 + j) * HEAD + half * HALF, HALF), HALF)
                o_ref[pl.ds(u * SUB + first, rows), out] = (value * share).astype(jnp.bfloat16)

    @pl.when(has_last)
    def _():
        for i in LAST:
            to_partner[i].wait_recv()

        def step(h):
            acc[h, 0] += mix(held1[h, 0], h, 1, 0, SUB)
            finish(h, 1, 0, SUB, mix(held1[h, 1], h, 1, 0, SUB))

        each_head(step)

    @pl.when(jnp.logical_not(has_last))
    def _():
        each_head(lambda h: finish(h, 1, 0, SUB, None))

    @pl.when(jnp.logical_not(has_before))
    def _():
        each_head(lambda h: finish(h, 0, 0, SUB, None))

    @pl.when(has_before)
    def _():
        for i in LAST:
            first, rows = PIECES[i][1:]
            to_near[i].wait_recv()
            pl.when(odd)(forward[i].start)
            for h in range(KEY_VALUE_HEADS):
                weight = held0[h, :, pl.ds(0, first + rows), pl.ds(first, rows)]
                mixed = mix(weight.reshape(2 * (first + rows), rows), h, 0, first, rows)
                if first:
                    acc[h, 0, :, pl.ds(0, first)] += mixed[:, :first]
                finish(h, 0, first, rows, mixed[:, first:])

    @pl.when(has_after)
    def _():
        for copy in [flags_near] + to_near[:2] + to_near[3:]:
            copy.wait_send()

    pl.when(sends_whole)(to_near[2].wait_send)
    for copy in (keys_short, weights):
        pl.when(gives_edge)(copy.wait_send)
    pl.when(takes_edge)(q_to_hub[0].wait_send)

    @pl.when(sends_partner)
    def _():
        for copy in [flags_partner] + to_partner:
            copy.wait_send()

    @pl.when(hub)
    def _():
        for copy in onward + q_onward[1:]:
            copy.wait_send()


def solution(mesh):
    count = mesh.shape["ctx"]
    inverse = 10000.0 ** (-(np.arange(HALF, dtype=np.float64) * (2.0 / HEAD)))
    angle = np.arange(ROWS, dtype=np.float64)[:, None] * inverse
    table = np.stack([np.cos(angle), np.sin(angle), 0 * angle + inverse]).astype(np.float32)

    def body(queries, keys, values, query_gain, key_gain, session_flags, valid_length):
        assert queries.shape[0] == ROWS and 2 * ROWS == WINDOW
        pinned = functools.partial(pltpu.with_memory_space_constraint, memory_space=pltpu.HBM)
        bf16, f32, i32 = jnp.bfloat16, jnp.float32, jnp.int32
        dma = pltpu.SemaphoreType.DMA
        heads, pieces = KEY_VALUE_HEADS, len(PIECES)
        mixed = pl.pallas_call(
            functools.partial(kernel, count),
            out_shape=pltpu.VMEM((ROWS, QUERY_HEADS * HEAD), bf16),
            in_specs=[pl.BlockSpec(memory_space=pltpu.HBM)] * 7,
            out_specs=pl.BlockSpec(memory_space=pltpu.VMEM),
            scratch_shapes=[
                pltpu.VMEM((ROWS, QUERY_HEADS * HEAD), bf16),
                pltpu.VMEM((ROWS, KEY_VALUE_HEADS * HEAD), bf16),
                pltpu.VMEM((3, ROWS, HALF), f32),
                pltpu.VMEM((1, HEAD), f32),
                pltpu.VMEM((1, HEAD), f32),
                pltpu.VMEM((3, ROWS, KEY_VALUE_HEADS * HEAD), bf16),
                pltpu.VMEM((3, ROWS, KEY_VALUE_HEADS * HEAD), bf16),
                pltpu.VMEM((heads, 2, ROWS, HEAD), bf16),
                pltpu.VMEM((3, 1, ROWS), i32),
                pltpu.VMEM((ROWS, 128), i32),
                pltpu.VMEM((heads, 2, 2, SUB, HEAD), f32),
                pltpu.VMEM((heads, 2, 2, SUB, 128), f32),
                pltpu.VMEM((heads, 2, SUB, SUB), bf16),
                pltpu.VMEM((heads, 2, 2 * SUB, SUB), bf16),
                pltpu.VMEM((len(AROUND), PIECES[UNIT][2], heads * HEAD), bf16),
                pltpu.VMEM((heads, 2, EDGE_ROWS, HEAD), bf16),
                pltpu.VMEM((len(TAKERS), heads, 2, EDGE_ROWS, HEAD), bf16),
                pltpu.VMEM((QUERY_HEADS // PACK, EDGE_ROWS, 128), bf16),
                pltpu.VMEM((QUERY_HEADS // PACK, EDGE_ROWS, 128), bf16),
                dma((7,)),
                dma((2,)),
                dma((2,)),
                dma((pieces + 1,)),
                dma((pieces + 1,)),
                dma((pieces,)),
                dma((pieces,)),
                dma((len(AROUND),)),
                dma((len(AROUND),)),
                dma((len(TAKERS),)),
                dma((len(TAKERS),)),
            ],
            compiler_params=pltpu.CompilerParams(
                collective_id=0, has_side_effects=True, vmem_limit_bytes=56 << 20
            ),
        )(
            pinned(queries),
            pinned(keys),
            pinned(values),
            pinned(query_gain.reshape(1, HEAD)),
            pinned(key_gain.reshape(1, HEAD)),
            pinned(session_flags.reshape(1, ROWS)),
            pinned(jnp.asarray(table)),
        )

        first = (count - 1) * ROWS

        def cut(mixed, limit):
            tick = first + lax.broadcasted_iota(i32, mixed.shape, 0)
            return jnp.where(tick < limit[0], mixed, jnp.zeros((), bf16))

        return lax.cond(
            lax.axis_index("ctx") == count - 1, cut, lambda mixed, limit: mixed, mixed, valid_length
        )

    return jax.shard_map(
        body,
        mesh=mesh,
        in_specs=(
            P(("dates", "ctx"), None),
            P(("dates", "ctx"), None),
            P(("dates", "ctx"), None),
            P(),
            P(),
            P(("dates", "ctx")),
            P("dates"),
        ),
        out_specs=P(("dates", "ctx"), None),
        check_vma=False,
    )
```

```python
import functools

import jax
import jax.numpy as jnp
import numpy as np
from jax import lax
from jax.experimental import pallas as pl
from jax.experimental.pallas import tpu as pltpu
from jax.sharding import PartitionSpec as P

QUERY_HEADS = 8
KEY_VALUE_HEADS = 4
HEAD = 256
HALF = HEAD // 2
WINDOW = 1024
ROWS = 512
SUB = 256
MESH = pl.DeviceIdType.MESH

PIECES = (
    ("v", 336, 176),
    ("k", 256, 256),
    ("k", 0, 256),
    ("v", 128, 128),
    ("v", 64, 64),
    ("v", 0, 64),
    ("v", 256, 80),
)
UNIT, WEIGHTS = 6, 7
EDGE_ROWS, BLOCK = 64, 32
PACK = 128 // BLOCK
BLOCKS = [
    (head, t, s) for head in range(QUERY_HEADS) for t in range(EDGE_ROWS // BLOCK) for s in range(t, EDGE_ROWS // BLOCK)
]
FIRST, LAST = (0, UNIT, 1), (3, 4, 5)
AROUND = (1, 3, 5)
TAKERS = (1, 3, 5, 7)


def kernel(
    count,
    q_hbm,
    k_hbm,
    v_hbm,
    q_gain_hbm,
    k_gain_hbm,
    flags_hbm,
    rope_hbm,
    o_ref,
    q_in,
    k_in,
    rope,
    q_gain,
    k_gain,
    kbuf,
    vbuf,
    qbuf,
    flags,
    low,
    acc,
    total,
    held0,
    held1,
    relay,
    q_edge,
    q_relay,
    w_out,
    w_in,
    load_sem,
    fsend_sem,
    frecv_sem,
    i_send,
    i_recv,
    d_send,
    d_recv,
    r_send,
    r_recv,
    q_send,
    q_recv,
):
    me = lax.axis_index("ctx")
    core = lax.rem(me, 2)
    even, odd = core == 0, core == 1
    chip = me // 2
    chips = count // 2
    near = lax.rem(me + 2, count)
    back = lax.rem(me + count - 2, count)
    partner = me + 1 - 2 * core
    has_after, has_before = chip < chips - 1, chip > 0
    forwards = odd & has_before
    sends_partner = even | has_before
    has_last = me > 0

    barrier = pltpu.get_barrier_semaphore()

    def ready(target):
        pl.semaphore_signal(barrier, inc=1, device_id={"ctx": target}, device_id_type=MESH)

    hub = me == 0
    around = [c for c in AROUND if c + 1 < chips]
    takers = [c for c in TAKERS if c < chips]

    def one_of(devices):
        return functools.reduce(jnp.logical_or, [me == d for d in devices], me < 0)

    goes_around = one_of([2 * c for c in around])
    takes_edge = one_of([2 * c for c in takers])
    gives_edge = one_of([2 * c - 2 for c in takers])

    pl.when(has_before)(lambda: ready(back))
    ready(partner)
    for c in takers:
        pl.when(hub)(functools.partial(ready, 2 * c))
    for c in around:
        pl.when(me == 2 * c + 2)(functools.partial(ready, 0))

    def span(index, width):
        return pl.ds(pl.multiple_of(index * width, width), width)

    def remote(src, dst, send, recv, target):
        return pltpu.make_async_remote_copy(
            src_ref=src,
            dst_ref=dst,
            send_sem=send,
            recv_sem=recv,
            device_id={"ctx": target},
            device_id_type=MESH,
        )

    loads = [
        pltpu.make_async_copy(src, dst, load_sem.at[i])
        for i, (src, dst) in enumerate(
            (
                (rope_hbm, rope),
                (k_hbm, k_in),
                (k_gain_hbm, k_gain),
                (q_hbm, q_in),
                (q_gain_hbm, q_gain),
                (v_hbm, vbuf.at[2]),
                (flags_hbm, flags.at[2]),
            )
        )
    ]
    for copy in loads:
        copy.start()
    load_r, load_k, load_kg, load_q, load_qg, load_v, load_f = loads

    def own(kind, first, rows):
        return (v_hbm if kind == "v" else kbuf.at[2]).at[pl.ds(first, rows)]

    def slot(kind, index, first, rows):
        return (vbuf if kind == "v" else kbuf).at[index, pl.ds(first, rows)]

    to_near, to_partner, forward = [], [], []
    for i, piece in enumerate(PIECES):
        to_near.append(remote(own(*piece), slot(piece[0], 0, *piece[1:]), i_send.at[i], i_recv.at[i], near))
        there = slot(piece[0], 1, *piece[1:])
        to_partner.append(remote(own(*piece), there, d_send.at[i], d_recv.at[i], partner))
        forward.append(
            remote(slot(piece[0], 0, *piece[1:]), there, d_send.at[i], d_recv.at[i], partner)
        )
    flags_near = remote(flags_hbm, flags.at[0], fsend_sem.at[0], frecv_sem.at[0], near)
    flags_partner = remote(flags_hbm, flags.at[1], fsend_sem.at[1], frecv_sem.at[1], partner)
    flags_forward = remote(flags.at[0], flags.at[1], fsend_sem.at[1], frecv_sem.at[1], partner)

    there = slot("v", 0, *PIECES[UNIT][1:])
    to_hub, onward = [], []
    for r, c in enumerate(around):
        to_hub.append(remote(own(*PIECES[UNIT]), relay.at[r], i_send.at[UNIT], r_recv.at[r], 0))
        onward.append(remote(relay.at[r], there, r_send.at[r], i_recv.at[UNIT], 2 * c + 2))

    q_rows = qbuf.at[:, :, pl.ds(0, EDGE_ROWS), :]
    q_to_hub, q_onward = [], []
    for r, c in enumerate(takers):
        target = q_relay.at[r] if r else q_edge
        q_to_hub.append(remote(q_rows, target, q_send.at[0], q_recv.at[r], 0))
        q_onward.append(remote(q_relay.at[r], q_edge, q_send.at[r], q_recv.at[0], 2 * c - 2))
    short = ("k", EDGE_ROWS, SUB - EDGE_ROWS)
    keys_short = remote(own(*short), slot("k", 0, *short[1:]), i_send.at[2], i_recv.at[2], near)
    weights = remote(w_out, w_in, i_send.at[WEIGHTS], i_recv.at[WEIGHTS], near)

    @pl.when(takes_edge)
    def _():
        kbuf[0, pl.ds(0, EDGE_ROWS), :] = jnp.zeros((EDGE_ROWS, KEY_VALUE_HEADS * HEAD), jnp.bfloat16)

    greetings = 1 + has_after.astype(jnp.int32) + takes_edge.astype(jnp.int32)
    pl.semaphore_wait(barrier, greetings + len(around) * hub.astype(jnp.int32))

    def start_all(condition, copies):
        @pl.when(condition)
        def _():
            for copy in copies:
                copy.start()

    start_all(has_after, [flags_near])
    start_all(has_after & odd, [to_near[i] for i in (0, UNIT)])
    for c, copy in zip(around, to_hub):
        start_all(me == 2 * c, [copy])
    start_all(even, [flags_partner] + [to_partner[i] for i in (0, UNIT) + LAST])

    load_r.wait()
    base = (me * ROWS).astype(jnp.float32) * rope[2, :8]
    base_cos, base_sin = jnp.cos(base)[:1], jnp.sin(base)[:1]
    row_cos, row_sin = rope[0], rope[1]
    rope[0] = base_cos * row_cos - base_sin * row_sin
    rope[1] = base_sin * row_cos + base_cos * row_sin

    def normed(raw, gain, rows, scale):
        x = raw.astype(jnp.float32)
        mean = jnp.sum(x * x, axis=-1, keepdims=True) * (1.0 / HEAD)
        x = x * lax.rsqrt(mean + 1e-06) * gain
        a, b = x[:, :HALF], x[:, HALF:]
        cosine, sine = rope[0, rows], rope[1, rows]
        first = (a * cosine - b * sine).astype(jnp.bfloat16)
        second = (b * cosine + a * sine).astype(jnp.bfloat16)
        if scale != 1.0:
            first, second = first * jnp.bfloat16(scale), second * jnp.bfloat16(scale)
        return first, second

    load_k.wait()
    load_kg.wait()
    for block, ready_pieces in ((SUB, (1,)), (0, (2,))):
        rows = pl.ds(block, SUB)
        for h in range(KEY_VALUE_HEADS):
            first, second = normed(k_in[rows, h * HEAD : (h + 1) * HEAD], k_gain[...], rows, 1.0)
            kbuf[2, rows, h * HEAD : h * HEAD + HALF] = first
            kbuf[2, rows, h * HEAD + HALF : (h + 1) * HEAD] = second
        start_all(has_after & odd, [to_near[i] for i in ready_pieces])
        start_all(even, [to_partner[i] for i in ready_pieces])
    start_all(has_after & odd, [to_near[i] for i in LAST])

    load_q.wait()
    load_qg.wait()

    def prepare(h, carry):
        for j in range(2):
            for u in range(2):
                rows = pl.ds(u * SUB, SUB)
                raw = q_in[rows, span(h * 2 + j, HEAD)]
                first, second = normed(raw, q_gain[...], rows, HEAD**-0.5)
                qbuf[h, j, rows, :HALF] = first
                qbuf[h, j, rows, HALF:] = second
        return carry

    lax.fori_loop(0, KEY_VALUE_HEADS, prepare, 0)
    for c, copy in zip(takers, q_to_hub):
        start_all(me == 2 * c, [copy])

    load_f.wait()

    @pl.when(has_before)
    def _():
        flags_near.wait_recv()

    start_all(forwards, [flags_forward])

    @pl.when(has_last)
    def _():
        flags_partner.wait_recv()

    @pl.when(jnp.logical_not(has_before))
    def _():
        flags[0] = jnp.zeros((1, ROWS), jnp.int32)

    @pl.when(jnp.logical_not(has_last))
    def _():
        flags[1] = jnp.zeros((1, ROWS), jnp.int32)

    first_tick = (me - 2) * ROWS
    column = lax.broadcasted_iota(jnp.int32, (1, ROWS), 1)

    def marks(index):
        place = column + index * ROWS
        return jnp.where((flags[index] == 1) & (place + first_tick >= 0), place, -first_tick)

    behind = jnp.max(jnp.maximum(marks(0), marks(1)), axis=1, keepdims=True)
    row = lax.broadcasted_iota(jnp.int32, (ROWS, ROWS), 0)
    col = lax.broadcasted_iota(jnp.int32, (ROWS, ROWS), 1)
    seen = jnp.where(col <= row, jnp.broadcast_to(marks(2), (ROWS, ROWS)), -first_tick)
    start = jnp.maximum(jnp.max(seen, axis=1, keepdims=True), behind)
    tick = lax.broadcasted_iota(jnp.int32, (ROWS, 1), 0) + WINDOW
    low[...] = jnp.broadcast_to(jnp.maximum(start, tick - (WINDOW - 1)), (ROWS, 128))

    def weigh(h, u, index, first, keys, least=None):
        ticks = pl.ds(u * SUB, SUB)
        q = qbuf[h, :, ticks, :].reshape(2 * SUB, HEAD)
        k = kbuf[index, pl.ds(first, keys), span(h, HEAD)]
        score = lax.dot_general(q, k, (((1,), (1,)), ((), ())), preferred_element_type=jnp.float32)
        offset = index * ROWS + first
        place = lax.broadcasted_iota(jnp.int32, (SUB, keys), 1) + offset
        allowed = place >= low[ticks][:, :1]
        if least is not None:
            allowed = allowed & (place >= least)
        if index == 2 and first + keys > u * SUB:
            tick = lax.broadcasted_iota(jnp.int32, (SUB, keys), 0) + (WINDOW + u * SUB)
            allowed = allowed & (place <= tick)
        weight = jnp.where(allowed[None], jnp.exp(score).reshape(2, SUB, keys), 0.0)
        weight = weight.reshape(2 * SUB, keys)
        lanes = weight[:, :128]
        for i in range(1, keys // 128):
            lanes = lanes + weight[:, i * 128 : (i + 1) * 128]
        return weight.astype(jnp.bfloat16), lanes.reshape(2, SUB, 128)

    def mix(weight, h, index, first, keys):
        v = vbuf[index, pl.ds(first, keys), span(h, HEAD)]
        mixed = jnp.dot(weight, v, preferred_element_type=jnp.float32)
        return mixed.reshape(2, weight.shape[0] // 2, HEAD)

    def part(h, u, index, first, keys, first_use=False):
        weight, lanes = weigh(h, u, index, first, keys)
        mixed = mix(weight, h, index, first, keys)
        if first_use:
            acc[h, u] = mixed
            total[h, u] = lanes
        else:
            acc[h, u] += mixed
            total[h, u] += lanes

    def each_head(step):
        lax.fori_loop(0, KEY_VALUE_HEADS, lambda h, carry: (step(h), carry)[1], 0)

    load_v.wait()

    def own_part(h):
        part(h, 0, 2, 0, SUB, True)
        part(h, 1, 2, 0, ROWS, True)

    each_head(own_part)

    @pl.when(hub)
    def _():
        for came, goes in zip(to_hub, onward):
            came.wait_recv()
            goes.start()
        for came, goes in zip(q_to_hub[1:], q_onward[1:]):
            came.wait_recv()
            goes.start()

    start_all(has_after & even & jnp.logical_not(goes_around), [to_near[UNIT]])
    start_all(has_after & even, to_near[:2])
    sends_whole = has_after & jnp.logical_not(gives_edge)
    start_all(even & sends_whole, [to_near[i] for i in (2,) + LAST])
    start_all(gives_edge, [keys_short])

    def receive(pieces):
        @pl.when(forwards)
        def _():
            for i in pieces:
                to_near[i].wait_recv()
                forward[i].start()

        @pl.when(has_last)
        def _():
            for i in pieces:
                to_partner[i].wait_recv()

    def receive_own(pieces):
        @pl.when(has_before & even)
        def _():
            for i in pieces:
                to_near[i].wait_recv()

    receive(FIRST)

    @pl.when(has_last)
    def _():
        def step(h):
            part(h, 0, 1, SUB, SUB)
            part(h, 1, 1, SUB, SUB)

        each_head(step)

    @pl.when(gives_edge)
    def _():
        q_to_hub[0].wait_recv()
        tick = lax.broadcasted_iota(jnp.int32, (EDGE_ROWS, 128), 0)
        place = lax.broadcasted_iota(jnp.int32, (EDGE_ROWS, 128), 1)
        packed = [jnp.zeros((BLOCK, 128), jnp.float32)] * (len(BLOCKS) // PACK)
        for head in range(QUERY_HEADS):
            h, j = divmod(head, 2)
            k = kbuf[2, :128, h * HEAD : (h + 1) * HEAD]
            score = lax.dot_general(
                q_edge[h, j], k, (((1,), (1,)), ((), ())), preferred_element_type=jnp.float32
            )
            weight = jnp.where((place > tick) & (place < EDGE_ROWS), jnp.exp(score), 0.0)
            for n, (owner, t, s) in enumerate(BLOCKS):
                if owner == head:
                    part_of = slice(t * BLOCK, (t + 1) * BLOCK)
                    block = jnp.where(place[part_of] // BLOCK == s, weight[part_of], 0.0)
                    shift = (n % PACK - s) * BLOCK % 128
                    packed[n // PACK] += pltpu.roll(block, shift, 1) if shift else block
        for g, block in enumerate(packed):
            w_out[g] = block.astype(jnp.bfloat16)
        weights.start()
        for i in LAST:
            to_near[i].start()

    receive_own(FIRST)

    @pl.when(has_before)
    def _():
        def step(h):
            part(h, 0, 0, SUB, SUB)
            part(h, 1, 0, SUB, SUB)

        each_head(step)

    receive((2,))

    @pl.when(has_last)
    def _():
        def step(h):
            for u in range(2):
                weight, lanes = weigh(h, u, 1, 0, SUB)
                held1[h, u] = weight
                total[h, u] += lanes

        each_head(step)

    pl.when(takes_edge)(keys_short.wait_recv)
    pl.when(has_before & even & jnp.logical_not(takes_edge))(to_near[2].wait_recv)

    least = jnp.where(takes_edge, EDGE_ROWS, 0)

    @pl.when(has_before)
    def _():
        def step(h):
            weight, lanes = weigh(h, 0, 0, 0, SUB, least)
            held0[h] = weight.reshape(2, SUB, SUB)
            total[h, 0] += lanes

        each_head(step)


    @pl.when(takes_edge)
    def _():
        weights.wait_recv()
        place = lax.broadcasted_iota(jnp.int32, (BLOCK, 128), 1)
        for n, (head, t, s) in enumerate(BLOCKS):
            h, j = divmod(head, 2)
            ticks = pl.ds(t * BLOCK, BLOCK)
            shift = (s - n % PACK) * BLOCK % 128
            weight = w_in[n // PACK].astype(jnp.float32)
            weight = pltpu.roll(weight, shift, 1) if shift else weight
            allowed = (place >= low[ticks]) & (place // BLOCK == s)
            weight = jnp.where(allowed, weight, 0.0)
            total[h, 0, j, ticks] += weight
            kept = held0[h, j, ticks, :128].astype(jnp.float32)
            held0[h, j, ticks, :128] = (kept + weight).astype(jnp.bfloat16)

    def divide(h):
        for u in range(2):
            for j in range(2):
                whole = jnp.sum(total[h, u, j], axis=-1, keepdims=True)
                share = 1.0 / whole
                total[h, u, j] = jnp.broadcast_to(share, (SUB, 128))

    each_head(divide)

    def finish(h, u, first, rows, mixed):
        ticks = pl.ds(first, rows)
        for j in range(2):
            share = total[h, u, j, ticks]
            for half in range(2):
                lanes = slice(half * HALF, (half + 1) * HALF)
                value = acc[h, u, j, ticks, lanes]
                if mixed is not None:
                    value = value + mixed[j, :, lanes]
                out = pl.ds(pl.multiple_of((h * 2 + j) * HEAD + half * HALF, HALF), HALF)
                o_ref[pl.ds(u * SUB + first, rows), out] = (value * share).astype(jnp.bfloat16)

    @pl.when(has_last)
    def _():
        for i in LAST:
            to_partner[i].wait_recv()

        def step(h):
            acc[h, 0] += mix(held1[h, 0], h, 1, 0, SUB)
            finish(h, 1, 0, SUB, mix(held1[h, 1], h, 1, 0, SUB))

        each_head(step)

    @pl.when(jnp.logical_not(has_last))
    def _():
        each_head(lambda h: finish(h, 1, 0, SUB, None))

    @pl.when(jnp.logical_not(has_before))
    def _():
        each_head(lambda h: finish(h, 0, 0, SUB, None))

    @pl.when(has_before)
    def _():
        for i in LAST:
            first, rows = PIECES[i][1:]
            to_near[i].wait_recv()
            pl.when(odd)(forward[i].start)
            for h in range(KEY_VALUE_HEADS):
                weight = held0[h, :, pl.ds(0, first + rows), pl.ds(first, rows)]
                mixed = mix(weight.reshape(2 * (first + rows), rows), h, 0, first, rows)
                if first:
                    acc[h, 0, :, pl.ds(0, first)] += mixed[:, :first]
                finish(h, 0, first, rows, mixed[:, first:])

    @pl.when(has_after)
    def _():
        for copy in [flags_near] + to_near[:2] + to_near[3:]:
            copy.wait_send()

    pl.when(sends_whole)(to_near[2].wait_send)
    for copy in (keys_short, weights):
        pl.when(gives_edge)(copy.wait_send)
    pl.when(takes_edge)(q_to_hub[0].wait_send)

    @pl.when(sends_partner)
    def _():
        for copy in [flags_partner] + to_partner:
            copy.wait_send()

    @pl.when(hub)
    def _():
        for copy in onward + q_onward[1:]:
            copy.wait_send()


def solution(mesh):
    count = mesh.shape["ctx"]
    inverse = 10000.0 ** (-(np.arange(HALF, dtype=np.float64) * (2.0 / HEAD)))
    angle = np.arange(ROWS, dtype=np.float64)[:, None] * inverse
    table = np.stack([np.cos(angle), np.sin(angle), 0 * angle + inverse]).astype(np.float32)

    def body(queries, keys, values, query_gain, key_gain, session_flags, valid_length):
        assert queries.shape[0] == ROWS and 2 * ROWS == WINDOW
        pinned = functools.partial(pltpu.with_memory_space_constraint, memory_space=pltpu.HBM)
        bf16, f32, i32 = jnp.bfloat16, jnp.float32, jnp.int32
        dma = pltpu.SemaphoreType.DMA
        heads, pieces = KEY_VALUE_HEADS, len(PIECES)
        mixed = pl.pallas_call(
            functools.partial(kernel, count),
            out_shape=pltpu.VMEM((ROWS, QUERY_HEADS * HEAD), bf16),
            in_specs=[pl.BlockSpec(memory_space=pltpu.HBM)] * 7,
            out_specs=pl.BlockSpec(memory_space=pltpu.VMEM),
            scratch_shapes=[
                pltpu.VMEM((ROWS, QUERY_HEADS * HEAD), bf16),
                pltpu.VMEM((ROWS, KEY_VALUE_HEADS * HEAD), bf16),
                pltpu.VMEM((3, ROWS, HALF), f32),
                pltpu.VMEM((1, HEAD), f32),
                pltpu.VMEM((1, HEAD), f32),
                pltpu.VMEM((3, ROWS, KEY_VALUE_HEADS * HEAD), bf16),
                pltpu.VMEM((3, ROWS, KEY_VALUE_HEADS * HEAD), bf16),
                pltpu.VMEM((heads, 2, ROWS, HEAD), bf16),
                pltpu.VMEM((3, 1, ROWS), i32),
                pltpu.VMEM((ROWS, 128), i32),
                pltpu.VMEM((heads, 2, 2, SUB, HEAD), f32),
                pltpu.VMEM((heads, 2, 2, SUB, 128), f32),
                pltpu.VMEM((heads, 2, SUB, SUB), bf16),
                pltpu.VMEM((heads, 2, 2 * SUB, SUB), bf16),
                pltpu.VMEM((len(AROUND), PIECES[UNIT][2], heads * HEAD), bf16),
                pltpu.VMEM((heads, 2, EDGE_ROWS, HEAD), bf16),
                pltpu.VMEM((len(TAKERS), heads, 2, EDGE_ROWS, HEAD), bf16),
                pltpu.VMEM((len(BLOCKS) // PACK, BLOCK, 128), bf16),
                pltpu.VMEM((len(BLOCKS) // PACK, BLOCK, 128), bf16),
                dma((7,)),
                dma((2,)),
                dma((2,)),
                dma((pieces + 1,)),
                dma((pieces + 1,)),
                dma((pieces,)),
                dma((pieces,)),
                dma((len(AROUND),)),
                dma((len(AROUND),)),
                dma((len(TAKERS),)),
                dma((len(TAKERS),)),
            ],
            compiler_params=pltpu.CompilerParams(
                collective_id=0, has_side_effects=True, vmem_limit_bytes=56 << 20
            ),
        )(
            pinned(queries),
            pinned(keys),
            pinned(values),
            pinned(query_gain.reshape(1, HEAD)),
            pinned(key_gain.reshape(1, HEAD)),
            pinned(session_flags.reshape(1, ROWS)),
            pinned(jnp.asarray(table)),
        )

        first = (count - 1) * ROWS

        def cut(mixed, limit):
            tick = first + lax.broadcasted_iota(i32, mixed.shape, 0)
            return jnp.where(tick < limit[0], mixed, jnp.zeros((), bf16))

        return lax.cond(
            lax.axis_index("ctx") == count - 1, cut, lambda mixed, limit: mixed, mixed, valid_length
        )

    return jax.shard_map(
        body,
        mesh=mesh,
        in_specs=(
            P(("dates", "ctx"), None),
            P(("dates", "ctx"), None),
            P(("dates", "ctx"), None),
            P(),
            P(),
            P(("dates", "ctx")),
            P("dates"),
        ),
        out_specs=P(("dates", "ctx"), None),
        check_vma=False,
    )
```

```python
import functools

import jax
import jax.numpy as jnp
import numpy as np
from jax import lax
from jax.experimental import pallas as pl
from jax.experimental.pallas import tpu as pltpu
from jax.sharding import PartitionSpec as P

QUERY_HEADS = 8
KEY_VALUE_HEADS = 4
HEAD = 256
HALF = HEAD // 2
WINDOW = 1024
ROWS = 512
SUB = 256
MESH = pl.DeviceIdType.MESH

PIECES = (
    ("v", 336, 176),
    ("k", 256, 256),
    ("k", 0, 256),
    ("v", 128, 128),
    ("v", 64, 64),
    ("v", 0, 64),
    ("v", 256, 80),
)
UNIT, WEIGHTS = 6, 7
EDGE_ROWS, BLOCK = 64, 32
PACK = 128 // BLOCK
BLOCKS = [
    (head, t, s) for head in range(QUERY_HEADS) for t in range(EDGE_ROWS // BLOCK) for s in range(t, EDGE_ROWS // BLOCK)
]
FIRST, LAST = (0, UNIT, 1), (3, 4, 5)
AROUND = (1, 3, 5)
TAKERS = (1, 3, 5, 7)


def kernel(
    count,
    q_hbm,
    k_hbm,
    v_hbm,
    q_gain_hbm,
    k_gain_hbm,
    flags_hbm,
    rope_hbm,
    o_ref,
    q_in,
    k_in,
    rope,
    q_gain,
    k_gain,
    kbuf,
    vbuf,
    qbuf,
    flags,
    low,
    acc,
    total,
    held0,
    held1,
    relay,
    q_edge,
    q_relay,
    w_out,
    w_in,
    load_sem,
    fsend_sem,
    frecv_sem,
    i_send,
    i_recv,
    d_send,
    d_recv,
    r_send,
    r_recv,
    q_send,
    q_recv,
):
    me = lax.axis_index("ctx")
    core = lax.rem(me, 2)
    even, odd = core == 0, core == 1
    chip = me // 2
    chips = count // 2
    near = lax.rem(me + 2, count)
    back = lax.rem(me + count - 2, count)
    partner = me + 1 - 2 * core
    has_after, has_before = chip < chips - 1, chip > 0
    forwards = odd & has_before
    sends_partner = even | has_before
    has_last = me > 0

    barrier = pltpu.get_barrier_semaphore()

    def ready(target):
        pl.semaphore_signal(barrier, inc=1, device_id={"ctx": target}, device_id_type=MESH)

    hub = me == 0
    around = [c for c in AROUND if c + 1 < chips]
    takers = [c for c in TAKERS if c < chips]

    def one_of(devices):
        return functools.reduce(jnp.logical_or, [me == d for d in devices], me < 0)

    goes_around = one_of([2 * c for c in around])
    takes_edge = one_of([2 * c for c in takers])
    gives_edge = one_of([2 * c - 2 for c in takers])

    pl.when(has_before)(lambda: ready(back))
    ready(partner)
    for c in takers:
        pl.when(hub)(functools.partial(ready, 2 * c))
    for c in around:
        pl.when(me == 2 * c + 2)(functools.partial(ready, 0))

    def span(index, width):
        return pl.ds(pl.multiple_of(index * width, width), width)

    def remote(src, dst, send, recv, target):
        return pltpu.make_async_remote_copy(
            src_ref=src,
            dst_ref=dst,
            send_sem=send,
            recv_sem=recv,
            device_id={"ctx": target},
            device_id_type=MESH,
        )

    loads = [
        pltpu.make_async_copy(src, dst, load_sem.at[i])
        for i, (src, dst) in enumerate(
            (
                (rope_hbm, rope),
                (k_hbm, k_in),
                (k_gain_hbm, k_gain),
                (q_hbm, q_in),
                (q_gain_hbm, q_gain),
                (v_hbm, vbuf.at[2]),
                (flags_hbm, flags.at[2]),
            )
        )
    ]
    for copy in loads:
        copy.start()
    load_r, load_k, load_kg, load_q, load_qg, load_v, load_f = loads

    def own(kind, first, rows):
        return (v_hbm if kind == "v" else kbuf.at[2]).at[pl.ds(first, rows)]

    def slot(kind, index, first, rows):
        return (vbuf if kind == "v" else kbuf).at[index, pl.ds(first, rows)]

    to_near, to_partner, forward = [], [], []
    for i, piece in enumerate(PIECES):
        to_near.append(remote(own(*piece), slot(piece[0], 0, *piece[1:]), i_send.at[i], i_recv.at[i], near))
        there = slot(piece[0], 1, *piece[1:])
        to_partner.append(remote(own(*piece), there, d_send.at[i], d_recv.at[i], partner))
        forward.append(
            remote(slot(piece[0], 0, *piece[1:]), there, d_send.at[i], d_recv.at[i], partner)
        )
    flags_near = remote(flags_hbm, flags.at[0], fsend_sem.at[0], frecv_sem.at[0], near)
    flags_partner = remote(flags_hbm, flags.at[1], fsend_sem.at[1], frecv_sem.at[1], partner)
    flags_forward = remote(flags.at[0], flags.at[1], fsend_sem.at[1], frecv_sem.at[1], partner)

    there = slot("v", 0, *PIECES[UNIT][1:])
    to_hub, onward = [], []
    for r, c in enumerate(around):
        to_hub.append(remote(own(*PIECES[UNIT]), relay.at[r], i_send.at[UNIT], r_recv.at[r], 0))
        onward.append(remote(relay.at[r], there, r_send.at[r], i_recv.at[UNIT], 2 * c + 2))

    q_rows = qbuf.at[:, :, pl.ds(0, EDGE_ROWS), :]
    q_to_hub, q_onward = [], []
    for r, c in enumerate(takers):
        target = q_relay.at[r] if r else q_edge
        q_to_hub.append(remote(q_rows, target, q_send.at[0], q_recv.at[r], 0))
        q_onward.append(remote(q_relay.at[r], q_edge, q_send.at[r], q_recv.at[0], 2 * c - 2))
    short = ("k", EDGE_ROWS, SUB - EDGE_ROWS)
    keys_short = remote(own(*short), slot("k", 0, *short[1:]), i_send.at[2], i_recv.at[2], near)
    weights = remote(w_out, w_in, i_send.at[WEIGHTS], i_recv.at[WEIGHTS], near)

    @pl.when(takes_edge)
    def _():
        kbuf[0, pl.ds(0, EDGE_ROWS), :] = jnp.zeros((EDGE_ROWS, KEY_VALUE_HEADS * HEAD), jnp.bfloat16)

    greetings = 1 + has_after.astype(jnp.int32) + takes_edge.astype(jnp.int32)
    pl.semaphore_wait(barrier, greetings + len(around) * hub.astype(jnp.int32))

    def start_all(condition, copies):
        @pl.when(condition)
        def _():
            for copy in copies:
                copy.start()

    start_all(has_after & odd, [to_near[i] for i in (0, UNIT)])
    start_all(has_after, [flags_near])
    for c, copy in zip(around, to_hub):
        start_all(me == 2 * c, [copy])
    start_all(even, [flags_partner] + [to_partner[i] for i in (0, UNIT) + LAST])

    load_r.wait()
    base = (me * ROWS).astype(jnp.float32) * rope[2, :8]
    base_cos, base_sin = jnp.cos(base)[:1], jnp.sin(base)[:1]
    row_cos, row_sin = rope[0], rope[1]
    rope[0] = base_cos * row_cos - base_sin * row_sin
    rope[1] = base_sin * row_cos + base_cos * row_sin

    def normed(raw, gain, rows, scale):
        x = raw.astype(jnp.float32)
        mean = jnp.sum(x * x, axis=-1, keepdims=True) * (1.0 / HEAD)
        x = x * lax.rsqrt(mean + 1e-06) * gain
        a, b = x[:, :HALF], x[:, HALF:]
        cosine, sine = rope[0, rows], rope[1, rows]
        first = (a * cosine - b * sine).astype(jnp.bfloat16)
        second = (b * cosine + a * sine).astype(jnp.bfloat16)
        if scale != 1.0:
            first, second = first * jnp.bfloat16(scale), second * jnp.bfloat16(scale)
        return first, second

    load_k.wait()
    load_kg.wait()
    for block, ready_pieces in ((SUB, (1,)), (0, (2,))):
        rows = pl.ds(block, SUB)
        for h in range(KEY_VALUE_HEADS):
            first, second = normed(k_in[rows, h * HEAD : (h + 1) * HEAD], k_gain[...], rows, 1.0)
            kbuf[2, rows, h * HEAD : h * HEAD + HALF] = first
            kbuf[2, rows, h * HEAD + HALF : (h + 1) * HEAD] = second
        start_all(has_after & odd, [to_near[i] for i in ready_pieces])
        start_all(even, [to_partner[i] for i in ready_pieces])
    start_all(has_after & odd, [to_near[i] for i in LAST])

    load_q.wait()
    load_qg.wait()

    def prepare(h, carry):
        for j in range(2):
            for u in range(2):
                rows = pl.ds(u * SUB, SUB)
                raw = q_in[rows, span(h * 2 + j, HEAD)]
                first, second = normed(raw, q_gain[...], rows, HEAD**-0.5)
                qbuf[h, j, rows, :HALF] = first
                qbuf[h, j, rows, HALF:] = second
        return carry

    lax.fori_loop(0, KEY_VALUE_HEADS, prepare, 0)
    for c, copy in zip(takers, q_to_hub):
        start_all(me == 2 * c, [copy])

    load_f.wait()

    @pl.when(has_before)
    def _():
        flags_near.wait_recv()

    start_all(forwards, [flags_forward])

    @pl.when(has_last)
    def _():
        flags_partner.wait_recv()

    @pl.when(jnp.logical_not(has_before))
    def _():
        flags[0] = jnp.zeros((1, ROWS), jnp.int32)

    @pl.when(jnp.logical_not(has_last))
    def _():
        flags[1] = jnp.zeros((1, ROWS), jnp.int32)

    first_tick = (me - 2) * ROWS
    column = lax.broadcasted_iota(jnp.int32, (1, ROWS), 1)

    def marks(index):
        place = column + index * ROWS
        return jnp.where((flags[index] == 1) & (place + first_tick >= 0), place, -first_tick)

    behind = jnp.max(jnp.maximum(marks(0), marks(1)), axis=1, keepdims=True)
    row = lax.broadcasted_iota(jnp.int32, (ROWS, ROWS), 0)
    col = lax.broadcasted_iota(jnp.int32, (ROWS, ROWS), 1)
    seen = jnp.where(col <= row, jnp.broadcast_to(marks(2), (ROWS, ROWS)), -first_tick)
    start = jnp.maximum(jnp.max(seen, axis=1, keepdims=True), behind)
    tick = lax.broadcasted_iota(jnp.int32, (ROWS, 1), 0) + WINDOW
    low[...] = jnp.broadcast_to(jnp.maximum(start, tick - (WINDOW - 1)), (ROWS, 128))

    def weigh(h, u, index, first, keys, least=None):
        ticks = pl.ds(u * SUB, SUB)
        q = qbuf[h, :, ticks, :].reshape(2 * SUB, HEAD)
        k = kbuf[index, pl.ds(first, keys), span(h, HEAD)]
        score = lax.dot_general(q, k, (((1,), (1,)), ((), ())), preferred_element_type=jnp.float32)
        offset = index * ROWS + first
        place = lax.broadcasted_iota(jnp.int32, (SUB, keys), 1) + offset
        allowed = place >= low[ticks][:, :1]
        if least is not None:
            allowed = allowed & (place >= least)
        if index == 2 and first + keys > u * SUB:
            tick = lax.broadcasted_iota(jnp.int32, (SUB, keys), 0) + (WINDOW + u * SUB)
            allowed = allowed & (place <= tick)
        weight = jnp.where(allowed[None], jnp.exp(score).reshape(2, SUB, keys), 0.0)
        weight = weight.reshape(2 * SUB, keys)
        lanes = weight[:, :128]
        for i in range(1, keys // 128):
            lanes = lanes + weight[:, i * 128 : (i + 1) * 128]
        return weight.astype(jnp.bfloat16), lanes.reshape(2, SUB, 128)

    def mix(weight, h, index, first, keys):
        v = vbuf[index, pl.ds(first, keys), span(h, HEAD)]
        mixed = jnp.dot(weight, v, preferred_element_type=jnp.float32)
        return mixed.reshape(2, weight.shape[0] // 2, HEAD)

    def part(h, u, index, first, keys, first_use=False):
        weight, lanes = weigh(h, u, index, first, keys)
        mixed = mix(weight, h, index, first, keys)
        if first_use:
            acc[h, u] = mixed
            total[h, u] = lanes
        else:
            acc[h, u] += mixed
            total[h, u] += lanes

    def each_head(step):
        lax.fori_loop(0, KEY_VALUE_HEADS, lambda h, carry: (step(h), carry)[1], 0)

    load_v.wait()

    def own_part(h):
        part(h, 0, 2, 0, SUB, True)
        part(h, 1, 2, 0, ROWS, True)

    each_head(own_part)

    @pl.when(hub)
    def _():
        for came, goes in zip(to_hub, onward):
            came.wait_recv()
            goes.start()
        for came, goes in zip(q_to_hub[1:], q_onward[1:]):
            came.wait_recv()
            goes.start()

    start_all(has_after & even & jnp.logical_not(goes_around), [to_near[UNIT]])
    start_all(has_after & even, to_near[:2])
    sends_whole = has_after & jnp.logical_not(gives_edge)
    start_all(even & sends_whole, [to_near[i] for i in (2,) + LAST])
    start_all(gives_edge, [keys_short])

    def receive(pieces):
        @pl.when(forwards)
        def _():
            for i in pieces:
                to_near[i].wait_recv()
                forward[i].start()

        @pl.when(has_last)
        def _():
            for i in pieces:
                to_partner[i].wait_recv()

    def receive_own(pieces):
        @pl.when(has_before & even)
        def _():
            for i in pieces:
                to_near[i].wait_recv()

    receive(FIRST)

    @pl.when(has_last)
    def _():
        def step(h):
            part(h, 0, 1, SUB, SUB)
            part(h, 1, 1, SUB, SUB)

        each_head(step)

    @pl.when(gives_edge)
    def _():
        q_to_hub[0].wait_recv()
        tick = lax.broadcasted_iota(jnp.int32, (EDGE_ROWS, 128), 0)
        place = lax.broadcasted_iota(jnp.int32, (EDGE_ROWS, 128), 1)
        packed = [jnp.zeros((BLOCK, 128), jnp.float32)] * (len(BLOCKS) // PACK)
        for head in range(QUERY_HEADS):
            h, j = divmod(head, 2)
            k = kbuf[2, :128, h * HEAD : (h + 1) * HEAD]
            score = lax.dot_general(
                q_edge[h, j], k, (((1,), (1,)), ((), ())), preferred_element_type=jnp.float32
            )
            weight = jnp.where((place > tick) & (place < EDGE_ROWS), jnp.exp(score), 0.0)
            for n, (owner, t, s) in enumerate(BLOCKS):
                if owner == head:
                    part_of = slice(t * BLOCK, (t + 1) * BLOCK)
                    block = jnp.where(place[part_of] // BLOCK == s, weight[part_of], 0.0)
                    shift = (n % PACK - s) * BLOCK % 128
                    packed[n // PACK] += pltpu.roll(block, shift, 1) if shift else block
        for g, block in enumerate(packed):
            w_out[g] = block.astype(jnp.bfloat16)
        weights.start()
        for i in LAST:
            to_near[i].start()

    receive_own(FIRST)

    @pl.when(has_before)
    def _():
        def step(h):
            part(h, 0, 0, SUB, SUB)
            part(h, 1, 0, SUB, SUB)

        each_head(step)

    receive((2,))

    @pl.when(has_last)
    def _():
        def step(h):
            for u in range(2):
                weight, lanes = weigh(h, u, 1, 0, SUB)
                held1[h, u] = weight
                total[h, u] += lanes

        each_head(step)

    pl.when(takes_edge)(keys_short.wait_recv)
    pl.when(has_before & even & jnp.logical_not(takes_edge))(to_near[2].wait_recv)

    least = jnp.where(takes_edge, EDGE_ROWS, 0)

    @pl.when(has_before)
    def _():
        def step(h):
            weight, lanes = weigh(h, 0, 0, 0, SUB, least)
            held0[h] = weight.reshape(2, SUB, SUB)
            total[h, 0] += lanes

        each_head(step)


    @pl.when(takes_edge)
    def _():
        weights.wait_recv()
        place = lax.broadcasted_iota(jnp.int32, (BLOCK, 128), 1)
        for n, (head, t, s) in enumerate(BLOCKS):
            h, j = divmod(head, 2)
            ticks = pl.ds(t * BLOCK, BLOCK)
            shift = (s - n % PACK) * BLOCK % 128
            weight = w_in[n // PACK].astype(jnp.float32)
            weight = pltpu.roll(weight, shift, 1) if shift else weight
            allowed = (place >= low[ticks]) & (place // BLOCK == s)
            weight = jnp.where(allowed, weight, 0.0)
            total[h, 0, j, ticks] += weight
            kept = held0[h, j, ticks, :128].astype(jnp.float32)
            held0[h, j, ticks, :128] = (kept + weight).astype(jnp.bfloat16)

    def divide(h):
        for u in range(2):
            for j in range(2):
                whole = jnp.sum(total[h, u, j], axis=-1, keepdims=True)
                share = 1.0 / whole
                total[h, u, j] = jnp.broadcast_to(share, (SUB, 128))

    each_head(divide)

    def finish(h, u, first, rows, mixed):
        ticks = pl.ds(first, rows)
        for j in range(2):
            share = total[h, u, j, ticks]
            for half in range(2):
                lanes = slice(half * HALF, (half + 1) * HALF)
                value = acc[h, u, j, ticks, lanes]
                if mixed is not None:
                    value = value + mixed[j, :, lanes]
                out = pl.ds(pl.multiple_of((h * 2 + j) * HEAD + half * HALF, HALF), HALF)
                o_ref[pl.ds(u * SUB + first, rows), out] = (value * share).astype(jnp.bfloat16)

    @pl.when(has_last)
    def _():
        for i in LAST:
            to_partner[i].wait_recv()

        def step(h):
            acc[h, 0] += mix(held1[h, 0], h, 1, 0, SUB)
            finish(h, 1, 0, SUB, mix(held1[h, 1], h, 1, 0, SUB))

        each_head(step)

    @pl.when(jnp.logical_not(has_last))
    def _():
        each_head(lambda h: finish(h, 1, 0, SUB, None))

    @pl.when(has_after)
    def _():
        for copy in [flags_near] + [to_near[i] for i in FIRST]:
            copy.wait_send()

    @pl.when(sends_partner)
    def _():
        for copy in [flags_partner] + [to_partner[i] for i in FIRST + (2,)]:
            copy.wait_send()

    @pl.when(even)
    def _():
        for i in LAST:
            to_partner[i].wait_send()

    pl.when(takes_edge)(q_to_hub[0].wait_send)

    @pl.when(hub)
    def _():
        for copy in onward + q_onward[1:]:
            copy.wait_send()

    @pl.when(jnp.logical_not(has_before))
    def _():
        each_head(lambda h: finish(h, 0, 0, SUB, None))

    @pl.when(has_before)
    def _():
        for i in LAST:
            first, rows = PIECES[i][1:]
            to_near[i].wait_recv()
            pl.when(odd)(forward[i].start)
            for h in range(KEY_VALUE_HEADS):
                weight = held0[h, :, pl.ds(0, first + rows), pl.ds(first, rows)]
                mixed = mix(weight.reshape(2 * (first + rows), rows), h, 0, first, rows)
                if first:
                    acc[h, 0, :, pl.ds(0, first)] += mixed[:, :first]
                finish(h, 0, first, rows, mixed[:, first:])

    @pl.when(has_after)
    def _():
        for i in LAST:
            to_near[i].wait_send()

    pl.when(sends_whole)(to_near[2].wait_send)
    for copy in (keys_short, weights):
        pl.when(gives_edge)(copy.wait_send)

    @pl.when(forwards)
    def _():
        for i in LAST:
            to_partner[i].wait_send()


def solution(mesh):
    count = mesh.shape["ctx"]
    inverse = 10000.0 ** (-(np.arange(HALF, dtype=np.float64) * (2.0 / HEAD)))
    angle = np.arange(ROWS, dtype=np.float64)[:, None] * inverse
    table = np.stack([np.cos(angle), np.sin(angle), 0 * angle + inverse]).astype(np.float32)

    def body(queries, keys, values, query_gain, key_gain, session_flags, valid_length):
        assert queries.shape[0] == ROWS and 2 * ROWS == WINDOW
        pinned = functools.partial(pltpu.with_memory_space_constraint, memory_space=pltpu.HBM)
        bf16, f32, i32 = jnp.bfloat16, jnp.float32, jnp.int32
        dma = pltpu.SemaphoreType.DMA
        heads, pieces = KEY_VALUE_HEADS, len(PIECES)
        mixed = pl.pallas_call(
            functools.partial(kernel, count),
            out_shape=pltpu.VMEM((ROWS, QUERY_HEADS * HEAD), bf16),
            in_specs=[pl.BlockSpec(memory_space=pltpu.HBM)] * 7,
            out_specs=pl.BlockSpec(memory_space=pltpu.VMEM),
            scratch_shapes=[
                pltpu.VMEM((ROWS, QUERY_HEADS * HEAD), bf16),
                pltpu.VMEM((ROWS, KEY_VALUE_HEADS * HEAD), bf16),
                pltpu.VMEM((3, ROWS, HALF), f32),
                pltpu.VMEM((1, HEAD), f32),
                pltpu.VMEM((1, HEAD), f32),
                pltpu.VMEM((3, ROWS, KEY_VALUE_HEADS * HEAD), bf16),
                pltpu.VMEM((3, ROWS, KEY_VALUE_HEADS * HEAD), bf16),
                pltpu.VMEM((heads, 2, ROWS, HEAD), bf16),
                pltpu.VMEM((3, 1, ROWS), i32),
                pltpu.VMEM((ROWS, 128), i32),
                pltpu.VMEM((heads, 2, 2, SUB, HEAD), f32),
                pltpu.VMEM((heads, 2, 2, SUB, 128), f32),
                pltpu.VMEM((heads, 2, SUB, SUB), bf16),
                pltpu.VMEM((heads, 2, 2 * SUB, SUB), bf16),
                pltpu.VMEM((len(AROUND), PIECES[UNIT][2], heads * HEAD), bf16),
                pltpu.VMEM((heads, 2, EDGE_ROWS, HEAD), bf16),
                pltpu.VMEM((len(TAKERS), heads, 2, EDGE_ROWS, HEAD), bf16),
                pltpu.VMEM((len(BLOCKS) // PACK, BLOCK, 128), bf16),
                pltpu.VMEM((len(BLOCKS) // PACK, BLOCK, 128), bf16),
                dma((7,)),
                dma((2,)),
                dma((2,)),
                dma((pieces + 1,)),
                dma((pieces + 1,)),
                dma((pieces,)),
                dma((pieces,)),
                dma((len(AROUND),)),
                dma((len(AROUND),)),
                dma((len(TAKERS),)),
                dma((len(TAKERS),)),
            ],
            compiler_params=pltpu.CompilerParams(
                collective_id=0, has_side_effects=True, vmem_limit_bytes=56 << 20
            ),
        )(
            pinned(queries),
            pinned(keys),
            pinned(values),
            pinned(query_gain.reshape(1, HEAD)),
            pinned(key_gain.reshape(1, HEAD)),
            pinned(session_flags.reshape(1, ROWS)),
            pinned(jnp.asarray(table)),
        )

        first = (count - 1) * ROWS

        def cut(mixed, limit):
            tick = first + lax.broadcasted_iota(i32, mixed.shape, 0)
            return jnp.where(tick < limit[0], mixed, jnp.zeros((), bf16))

        return lax.cond(
            lax.axis_index("ctx") == count - 1, cut, lambda mixed, limit: mixed, mixed, valid_length
        )

    return jax.shard_map(
        body,
        mesh=mesh,
        in_specs=(
            P(("dates", "ctx"), None),
            P(("dates", "ctx"), None),
            P(("dates", "ctx"), None),
            P(),
            P(),
            P(("dates", "ctx")),
            P("dates"),
        ),
        out_specs=P(("dates", "ctx"), None),
        check_vma=False,
    )
```

```python
import functools

import jax
import jax.numpy as jnp
import numpy as np
from jax import lax
from jax.experimental import pallas as pl
from jax.experimental.pallas import tpu as pltpu
from jax.sharding import PartitionSpec as P

QUERY_HEADS = 8
KEY_VALUE_HEADS = 4
HEAD = 256
HALF = HEAD // 2
WINDOW = 1024
ROWS = 512
SUB = 256
MESH = pl.DeviceIdType.MESH

PIECES = (
    ("v", 352, 160),
    ("k", 256, 256),
    ("k", 0, 256),
    ("v", 128, 128),
    ("v", 64, 64),
    ("v", 0, 64),
    ("v", 256, 96),
)
UNIT, WEIGHTS = 6, 7
EDGE_ROWS, BLOCK = 64, 32
PACK = 128 // BLOCK
BLOCKS = [
    (head, t, s) for head in range(QUERY_HEADS) for t in range(EDGE_ROWS // BLOCK) for s in range(t, EDGE_ROWS // BLOCK)
]
FIRST, LAST = (0, UNIT, 1), (3, 4, 5)
AROUND = (1, 3, 5)
TAKERS = (1, 3, 5, 7)


def kernel(
    count,
    q_hbm,
    k_hbm,
    v_hbm,
    q_gain_hbm,
    k_gain_hbm,
    flags_hbm,
    rope_hbm,
    o_ref,
    q_in,
    k_in,
    rope,
    q_gain,
    k_gain,
    kbuf,
    vbuf,
    qbuf,
    flags,
    low,
    acc,
    total,
    held0,
    held1,
    relay,
    q_edge,
    q_relay,
    w_out,
    w_in,
    load_sem,
    fsend_sem,
    frecv_sem,
    i_send,
    i_recv,
    d_send,
    d_recv,
    r_send,
    r_recv,
    q_send,
    q_recv,
):
    me = lax.axis_index("ctx")
    core = lax.rem(me, 2)
    even, odd = core == 0, core == 1
    chip = me // 2
    chips = count // 2
    near = lax.rem(me + 2, count)
    back = lax.rem(me + count - 2, count)
    partner = me + 1 - 2 * core
    has_after, has_before = chip < chips - 1, chip > 0
    forwards = odd & has_before
    sends_partner = even | has_before
    has_last = me > 0

    barrier = pltpu.get_barrier_semaphore()

    def ready(target):
        pl.semaphore_signal(barrier, inc=1, device_id={"ctx": target}, device_id_type=MESH)

    hub = me == 0
    around = [c for c in AROUND if c + 1 < chips]
    takers = [c for c in TAKERS if c < chips]

    def one_of(devices):
        return functools.reduce(jnp.logical_or, [me == d for d in devices], me < 0)

    goes_around = one_of([2 * c for c in around])
    takes_edge = one_of([2 * c for c in takers])
    gives_edge = one_of([2 * c - 2 for c in takers])

    pl.when(has_before)(lambda: ready(back))
    ready(partner)
    for c in takers:
        pl.when(hub)(functools.partial(ready, 2 * c))
    for c in around:
        pl.when(me == 2 * c + 2)(functools.partial(ready, 0))

    def span(index, width):
        return pl.ds(pl.multiple_of(index * width, width), width)

    def remote(src, dst, send, recv, target):
        return pltpu.make_async_remote_copy(
            src_ref=src,
            dst_ref=dst,
            send_sem=send,
            recv_sem=recv,
            device_id={"ctx": target},
            device_id_type=MESH,
        )

    loads = [
        pltpu.make_async_copy(src, dst, load_sem.at[i])
        for i, (src, dst) in enumerate(
            (
                (rope_hbm, rope),
                (k_hbm, k_in),
                (k_gain_hbm, k_gain),
                (q_hbm, q_in),
                (q_gain_hbm, q_gain),
                (v_hbm, vbuf.at[2]),
                (flags_hbm, flags.at[2]),
            )
        )
    ]
    for copy in loads:
        copy.start()
    load_r, load_k, load_kg, load_q, load_qg, load_v, load_f = loads

    def own(kind, first, rows):
        return (v_hbm if kind == "v" else kbuf.at[2]).at[pl.ds(first, rows)]

    def slot(kind, index, first, rows):
        return (vbuf if kind == "v" else kbuf).at[index, pl.ds(first, rows)]

    to_near, to_partner, forward = [], [], []
    for i, piece in enumerate(PIECES):
        to_near.append(remote(own(*piece), slot(piece[0], 0, *piece[1:]), i_send.at[i], i_recv.at[i], near))
        there = slot(piece[0], 1, *piece[1:])
        to_partner.append(remote(own(*piece), there, d_send.at[i], d_recv.at[i], partner))
        forward.append(
            remote(slot(piece[0], 0, *piece[1:]), there, d_send.at[i], d_recv.at[i], partner)
        )
    flags_near = remote(flags_hbm, flags.at[0], fsend_sem.at[0], frecv_sem.at[0], near)
    flags_partner = remote(flags_hbm, flags.at[1], fsend_sem.at[1], frecv_sem.at[1], partner)
    flags_forward = remote(flags.at[0], flags.at[1], fsend_sem.at[1], frecv_sem.at[1], partner)

    there = slot("v", 0, *PIECES[UNIT][1:])
    to_hub, onward = [], []
    for r, c in enumerate(around):
        to_hub.append(remote(own(*PIECES[UNIT]), relay.at[r], i_send.at[UNIT], r_recv.at[r], 0))
        onward.append(remote(relay.at[r], there, r_send.at[r], i_recv.at[UNIT], 2 * c + 2))

    q_rows = qbuf.at[:, :, pl.ds(0, EDGE_ROWS), :]
    q_to_hub, q_onward = [], []
    for r, c in enumerate(takers):
        target = q_relay.at[r] if r else q_edge
        q_to_hub.append(remote(q_rows, target, q_send.at[0], q_recv.at[r], 0))
        q_onward.append(remote(q_relay.at[r], q_edge, q_send.at[r], q_recv.at[0], 2 * c - 2))
    short = ("k", EDGE_ROWS, SUB - EDGE_ROWS)
    keys_short = remote(own(*short), slot("k", 0, *short[1:]), i_send.at[2], i_recv.at[2], near)
    weights = remote(w_out, w_in, i_send.at[WEIGHTS], i_recv.at[WEIGHTS], near)

    @pl.when(takes_edge)
    def _():
        kbuf[0, pl.ds(0, EDGE_ROWS), :] = jnp.zeros((EDGE_ROWS, KEY_VALUE_HEADS * HEAD), jnp.bfloat16)

    greetings = 1 + has_after.astype(jnp.int32) + takes_edge.astype(jnp.int32)
    pl.semaphore_wait(barrier, greetings + len(around) * hub.astype(jnp.int32))

    def start_all(condition, copies):
        @pl.when(condition)
        def _():
            for copy in copies:
                copy.start()

    start_all(has_after & odd, [to_near[i] for i in (0, UNIT)])
    start_all(has_after, [flags_near])
    for c, copy in zip(around, to_hub):
        start_all(me == 2 * c, [copy])
    start_all(even, [flags_partner] + [to_partner[i] for i in (0, UNIT) + LAST])

    load_r.wait()
    base = (me * ROWS).astype(jnp.float32) * rope[2, :8]
    base_cos, base_sin = jnp.cos(base)[:1], jnp.sin(base)[:1]
    row_cos, row_sin = rope[0], rope[1]
    rope[0] = base_cos * row_cos - base_sin * row_sin
    rope[1] = base_sin * row_cos + base_cos * row_sin

    def normed(raw, gain, rows, scale):
        x = raw.astype(jnp.float32)
        mean = jnp.sum(x * x, axis=-1, keepdims=True) * (1.0 / HEAD)
        x = x * lax.rsqrt(mean + 1e-06) * gain
        a, b = x[:, :HALF], x[:, HALF:]
        cosine, sine = rope[0, rows], rope[1, rows]
        first = (a * cosine - b * sine).astype(jnp.bfloat16)
        second = (b * cosine + a * sine).astype(jnp.bfloat16)
        if scale != 1.0:
            first, second = first * jnp.bfloat16(scale), second * jnp.bfloat16(scale)
        return first, second

    load_k.wait()
    load_kg.wait()
    for block, ready_pieces in ((SUB, (1,)), (0, (2,))):
        rows = pl.ds(block, SUB)
        for h in range(KEY_VALUE_HEADS):
            first, second = normed(k_in[rows, h * HEAD : (h + 1) * HEAD], k_gain[...], rows, 1.0)
            kbuf[2, rows, h * HEAD : h * HEAD + HALF] = first
            kbuf[2, rows, h * HEAD + HALF : (h + 1) * HEAD] = second
        start_all(has_after & odd, [to_near[i] for i in ready_pieces])
        start_all(even, [to_partner[i] for i in ready_pieces])
    start_all(has_after & odd, [to_near[i] for i in LAST])

    load_q.wait()
    load_qg.wait()

    def prepare(h, carry):
        for j in range(2):
            for u in range(2):
                rows = pl.ds(u * SUB, SUB)
                raw = q_in[rows, span(h * 2 + j, HEAD)]
                first, second = normed(raw, q_gain[...], rows, HEAD**-0.5)
                qbuf[h, j, rows, :HALF] = first
                qbuf[h, j, rows, HALF:] = second
        return carry

    lax.fori_loop(0, KEY_VALUE_HEADS, prepare, 0)
    for c, copy in zip(takers, q_to_hub):
        start_all(me == 2 * c, [copy])

    load_f.wait()

    @pl.when(has_before)
    def _():
        flags_near.wait_recv()

    start_all(forwards, [flags_forward])

    @pl.when(has_last)
    def _():
        flags_partner.wait_recv()

    @pl.when(jnp.logical_not(has_before))
    def _():
        flags[0] = jnp.zeros((1, ROWS), jnp.int32)

    @pl.when(jnp.logical_not(has_last))
    def _():
        flags[1] = jnp.zeros((1, ROWS), jnp.int32)

    first_tick = (me - 2) * ROWS
    column = lax.broadcasted_iota(jnp.int32, (1, ROWS), 1)

    def marks(index):
        place = column + index * ROWS
        return jnp.where((flags[index] == 1) & (place + first_tick >= 0), place, -first_tick)

    behind = jnp.max(jnp.maximum(marks(0), marks(1)), axis=1, keepdims=True)
    row = lax.broadcasted_iota(jnp.int32, (ROWS, ROWS), 0)
    col = lax.broadcasted_iota(jnp.int32, (ROWS, ROWS), 1)
    seen = jnp.where(col <= row, jnp.broadcast_to(marks(2), (ROWS, ROWS)), -first_tick)
    start = jnp.maximum(jnp.max(seen, axis=1, keepdims=True), behind)
    tick = lax.broadcasted_iota(jnp.int32, (ROWS, 1), 0) + WINDOW
    low[...] = jnp.broadcast_to(jnp.maximum(start, tick - (WINDOW - 1)), (ROWS, 128))

    def weigh(h, u, index, first, keys, least=None):
        ticks = pl.ds(u * SUB, SUB)
        q = qbuf[h, :, ticks, :].reshape(2 * SUB, HEAD)
        k = kbuf[index, pl.ds(first, keys), span(h, HEAD)]
        score = lax.dot_general(q, k, (((1,), (1,)), ((), ())), preferred_element_type=jnp.float32)
        offset = index * ROWS + first
        place = lax.broadcasted_iota(jnp.int32, (SUB, keys), 1) + offset
        allowed = place >= low[ticks][:, :1]
        if least is not None:
            allowed = allowed & (place >= least)
        if index == 2 and first + keys > u * SUB:
            tick = lax.broadcasted_iota(jnp.int32, (SUB, keys), 0) + (WINDOW + u * SUB)
            allowed = allowed & (place <= tick)
        weight = jnp.where(allowed[None], jnp.exp(score).reshape(2, SUB, keys), 0.0)
        weight = weight.reshape(2 * SUB, keys)
        lanes = weight[:, :128]
        for i in range(1, keys // 128):
            lanes = lanes + weight[:, i * 128 : (i + 1) * 128]
        return weight.astype(jnp.bfloat16), lanes.reshape(2, SUB, 128)

    def mix(weight, h, index, first, keys):
        v = vbuf[index, pl.ds(first, keys), span(h, HEAD)]
        mixed = jnp.dot(weight, v, preferred_element_type=jnp.float32)
        return mixed.reshape(2, weight.shape[0] // 2, HEAD)

    def part(h, u, index, first, keys, first_use=False):
        weight, lanes = weigh(h, u, index, first, keys)
        mixed = mix(weight, h, index, first, keys)
        if first_use:
            acc[h, u] = mixed
            total[h, u] = lanes
        else:
            acc[h, u] += mixed
            total[h, u] += lanes

    def each_head(step):
        lax.fori_loop(0, KEY_VALUE_HEADS, lambda h, carry: (step(h), carry)[1], 0)

    load_v.wait()

    def own_part(h):
        part(h, 0, 2, 0, SUB, True)
        part(h, 1, 2, 0, ROWS, True)

    each_head(own_part)

    @pl.when(hub)
    def _():
        for came, goes in zip(to_hub, onward):
            came.wait_recv()
            goes.start()
        for came, goes in zip(q_to_hub[1:], q_onward[1:]):
            came.wait_recv()
            goes.start()

    start_all(has_after & even & jnp.logical_not(goes_around), [to_near[UNIT]])
    start_all(has_after & even, to_near[:2])
    sends_whole = has_after & jnp.logical_not(gives_edge)
    start_all(even & sends_whole, [to_near[i] for i in (2,) + LAST])
    start_all(gives_edge, [keys_short])

    def receive(pieces):
        @pl.when(forwards)
        def _():
            for i in pieces:
                to_near[i].wait_recv()
                forward[i].start()

        @pl.when(has_last)
        def _():
            for i in pieces:
                to_partner[i].wait_recv()

    def receive_own(pieces):
        @pl.when(has_before & even)
        def _():
            for i in pieces:
                to_near[i].wait_recv()

    receive(FIRST)

    @pl.when(has_last)
    def _():
        def step(h):
            part(h, 0, 1, SUB, SUB)
            part(h, 1, 1, SUB, SUB)

        each_head(step)

    @pl.when(gives_edge)
    def _():
        q_to_hub[0].wait_recv()
        tick = lax.broadcasted_iota(jnp.int32, (EDGE_ROWS, 128), 0)
        place = lax.broadcasted_iota(jnp.int32, (EDGE_ROWS, 128), 1)
        packed = [jnp.zeros((BLOCK, 128), jnp.float32)] * (len(BLOCKS) // PACK)
        for head in range(QUERY_HEADS):
            h, j = divmod(head, 2)
            k = kbuf[2, :128, h * HEAD : (h + 1) * HEAD]
            score = lax.dot_general(
                q_edge[h, j], k, (((1,), (1,)), ((), ())), preferred_element_type=jnp.float32
            )
            weight = jnp.where((place > tick) & (place < EDGE_ROWS), jnp.exp(score), 0.0)
            for n, (owner, t, s) in enumerate(BLOCKS):
                if owner == head:
                    part_of = slice(t * BLOCK, (t + 1) * BLOCK)
                    block = jnp.where(place[part_of] // BLOCK == s, weight[part_of], 0.0)
                    shift = (n % PACK - s) * BLOCK % 128
                    packed[n // PACK] += pltpu.roll(block, shift, 1) if shift else block
        for g, block in enumerate(packed):
            w_out[g] = block.astype(jnp.bfloat16)
        weights.start()
        for i in LAST:
            to_near[i].start()

    receive_own(FIRST)

    @pl.when(has_before)
    def _():
        def step(h):
            part(h, 0, 0, SUB, SUB)
            part(h, 1, 0, SUB, SUB)

        each_head(step)

    receive((2,))

    @pl.when(has_last)
    def _():
        def step(h):
            for u in range(2):
                weight, lanes = weigh(h, u, 1, 0, SUB)
                held1[h, u] = weight
                total[h, u] += lanes

        each_head(step)

    pl.when(takes_edge)(keys_short.wait_recv)
    pl.when(has_before & even & jnp.logical_not(takes_edge))(to_near[2].wait_recv)

    least = jnp.where(takes_edge, EDGE_ROWS, 0)

    @pl.when(has_before)
    def _():
        def step(h):
            weight, lanes = weigh(h, 0, 0, 0, SUB, least)
            held0[h] = weight.reshape(2, SUB, SUB)
            total[h, 0] += lanes

        each_head(step)


    @pl.when(takes_edge)
    def _():
        weights.wait_recv()
        place = lax.broadcasted_iota(jnp.int32, (BLOCK, 128), 1)
        for n, (head, t, s) in enumerate(BLOCKS):
            h, j = divmod(head, 2)
            ticks = pl.ds(t * BLOCK, BLOCK)
            shift = (s - n % PACK) * BLOCK % 128
            weight = w_in[n // PACK].astype(jnp.float32)
            weight = pltpu.roll(weight, shift, 1) if shift else weight
            allowed = (place >= low[ticks]) & (place // BLOCK == s)
            weight = jnp.where(allowed, weight, 0.0)
            total[h, 0, j, ticks] += weight
            kept = held0[h, j, ticks, :128].astype(jnp.float32)
            held0[h, j, ticks, :128] = (kept + weight).astype(jnp.bfloat16)

    def divide(h):
        for u in range(2):
            for j in range(2):
                whole = jnp.sum(total[h, u, j], axis=-1, keepdims=True)
                share = 1.0 / whole
                total[h, u, j] = jnp.broadcast_to(share, (SUB, 128))

    each_head(divide)

    def finish(h, u, first, rows, mixed):
        ticks = pl.ds(first, rows)
        for j in range(2):
            share = total[h, u, j, ticks]
            for half in range(2):
                lanes = slice(half * HALF, (half + 1) * HALF)
                value = acc[h, u, j, ticks, lanes]
                if mixed is not None:
                    value = value + mixed[j, :, lanes]
                out = pl.ds(pl.multiple_of((h * 2 + j) * HEAD + half * HALF, HALF), HALF)
                o_ref[pl.ds(u * SUB + first, rows), out] = (value * share).astype(jnp.bfloat16)

    @pl.when(has_last)
    def _():
        for i in LAST:
            to_partner[i].wait_recv()

        def step(h):
            acc[h, 0] += mix(held1[h, 0], h, 1, 0, SUB)
            finish(h, 1, 0, SUB, mix(held1[h, 1], h, 1, 0, SUB))

        each_head(step)

    @pl.when(jnp.logical_not(has_last))
    def _():
        each_head(lambda h: finish(h, 1, 0, SUB, None))

    @pl.when(has_after)
    def _():
        for copy in [flags_near] + [to_near[i] for i in FIRST]:
            copy.wait_send()

    @pl.when(sends_partner)
    def _():
        for copy in [flags_partner] + [to_partner[i] for i in FIRST + (2,)]:
            copy.wait_send()

    @pl.when(even)
    def _():
        for i in LAST:
            to_partner[i].wait_send()

    pl.when(takes_edge)(q_to_hub[0].wait_send)

    @pl.when(hub)
    def _():
        for copy in onward + q_onward[1:]:
            copy.wait_send()

    @pl.when(jnp.logical_not(has_before))
    def _():
        each_head(lambda h: finish(h, 0, 0, SUB, None))

    @pl.when(has_before)
    def _():
        for i in LAST:
            first, rows = PIECES[i][1:]
            to_near[i].wait_recv()
            pl.when(odd)(forward[i].start)
            for h in range(KEY_VALUE_HEADS):
                weight = held0[h, :, pl.ds(0, first + rows), pl.ds(first, rows)]
                mixed = mix(weight.reshape(2 * (first + rows), rows), h, 0, first, rows)
                if first:
                    acc[h, 0, :, pl.ds(0, first)] += mixed[:, :first]
                finish(h, 0, first, rows, mixed[:, first:])

    @pl.when(has_after)
    def _():
        for i in LAST:
            to_near[i].wait_send()

    pl.when(sends_whole)(to_near[2].wait_send)
    for copy in (keys_short, weights):
        pl.when(gives_edge)(copy.wait_send)

    @pl.when(forwards)
    def _():
        for i in LAST:
            to_partner[i].wait_send()


def solution(mesh):
    count = mesh.shape["ctx"]
    inverse = 10000.0 ** (-(np.arange(HALF, dtype=np.float64) * (2.0 / HEAD)))
    angle = np.arange(ROWS, dtype=np.float64)[:, None] * inverse
    table = np.stack([np.cos(angle), np.sin(angle), 0 * angle + inverse]).astype(np.float32)

    def body(queries, keys, values, query_gain, key_gain, session_flags, valid_length):
        assert queries.shape[0] == ROWS and 2 * ROWS == WINDOW
        pinned = functools.partial(pltpu.with_memory_space_constraint, memory_space=pltpu.HBM)
        bf16, f32, i32 = jnp.bfloat16, jnp.float32, jnp.int32
        dma = pltpu.SemaphoreType.DMA
        heads, pieces = KEY_VALUE_HEADS, len(PIECES)
        mixed = pl.pallas_call(
            functools.partial(kernel, count),
            out_shape=pltpu.VMEM((ROWS, QUERY_HEADS * HEAD), bf16),
            in_specs=[pl.BlockSpec(memory_space=pltpu.HBM)] * 7,
            out_specs=pl.BlockSpec(memory_space=pltpu.VMEM),
            scratch_shapes=[
                pltpu.VMEM((ROWS, QUERY_HEADS * HEAD), bf16),
                pltpu.VMEM((ROWS, KEY_VALUE_HEADS * HEAD), bf16),
                pltpu.VMEM((3, ROWS, HALF), f32),
                pltpu.VMEM((1, HEAD), f32),
                pltpu.VMEM((1, HEAD), f32),
                pltpu.VMEM((3, ROWS, KEY_VALUE_HEADS * HEAD), bf16),
                pltpu.VMEM((3, ROWS, KEY_VALUE_HEADS * HEAD), bf16),
                pltpu.VMEM((heads, 2, ROWS, HEAD), bf16),
                pltpu.VMEM((3, 1, ROWS), i32),
                pltpu.VMEM((ROWS, 128), i32),
                pltpu.VMEM((heads, 2, 2, SUB, HEAD), f32),
                pltpu.VMEM((heads, 2, 2, SUB, 128), f32),
                pltpu.VMEM((heads, 2, SUB, SUB), bf16),
                pltpu.VMEM((heads, 2, 2 * SUB, SUB), bf16),
                pltpu.VMEM((len(AROUND), PIECES[UNIT][2], heads * HEAD), bf16),
                pltpu.VMEM((heads, 2, EDGE_ROWS, HEAD), bf16),
                pltpu.VMEM((len(TAKERS), heads, 2, EDGE_ROWS, HEAD), bf16),
                pltpu.VMEM((len(BLOCKS) // PACK, BLOCK, 128), bf16),
                pltpu.VMEM((len(BLOCKS) // PACK, BLOCK, 128), bf16),
                dma((7,)),
                dma((2,)),
                dma((2,)),
                dma((pieces + 1,)),
                dma((pieces + 1,)),
                dma((pieces,)),
                dma((pieces,)),
                dma((len(AROUND),)),
                dma((len(AROUND),)),
                dma((len(TAKERS),)),
                dma((len(TAKERS),)),
            ],
            compiler_params=pltpu.CompilerParams(
                collective_id=0, has_side_effects=True, vmem_limit_bytes=56 << 20
            ),
        )(
            pinned(queries),
            pinned(keys),
            pinned(values),
            pinned(query_gain.reshape(1, HEAD)),
            pinned(key_gain.reshape(1, HEAD)),
            pinned(session_flags.reshape(1, ROWS)),
            pinned(jnp.asarray(table)),
        )

        first = (count - 1) * ROWS

        def cut(mixed, limit):
            tick = first + lax.broadcasted_iota(i32, mixed.shape, 0)
            return jnp.where(tick < limit[0], mixed, jnp.zeros((), bf16))

        return lax.cond(
            lax.axis_index("ctx") == count - 1, cut, lambda mixed, limit: mixed, mixed, valid_length
        )

    return jax.shard_map(
        body,
        mesh=mesh,
        in_specs=(
            P(("dates", "ctx"), None),
            P(("dates", "ctx"), None),
            P(("dates", "ctx"), None),
            P(),
            P(),
            P(("dates", "ctx")),
            P("dates"),
        ),
        out_specs=P(("dates", "ctx"), None),
        check_vma=False,
    )
```
